32 devices in a mesh: seq: 8 (over z, x), mp: 2 (over y), expert: 2 (over core).
Axes of the slice: x: 2, y: 2, z: 4, core: 2. Of those that a mesh axis runs over, the one named last changes fastest.
Arguments:
- hidden_prefix: bfloat16 [4480, 2048], P('seq'), may hold values from -6 to 6
- hidden_action: bfloat16 [800, 1024], P('seq'), may hold values from -6 to 6
- norm1_prefix: bfloat16 [2048], P('seq'), may hold values from 0.5 to 1.5
- query_prefix: bfloat16 [2048, 2048], P('seq', ('mp', 'expert')), may hold values from -0.125 to 0.125
- key_prefix: bfloat16 [2048, 256], P('seq'), may hold values from -0.125 to 0.125
- value_prefix: bfloat16 [2048, 256], P('seq'), may hold values from -0.125 to 0.125
- out_prefix: bfloat16 [2048, 2048], P(('mp', 'expert'), 'seq'), may hold values from -2 to 2
- norm2_prefix: bfloat16 [2048], P('seq'), may hold values from 0.5 to 1.5
- gate_prefix: bfloat16 [2048, 16384], P('seq', ('mp', 'expert')), may hold values from -0.125 to 0.125
- up_prefix: bfloat16 [2048, 16384], P('seq', ('mp', 'expert')), may hold values from -0.125 to 0.125
- down_prefix: bfloat16 [16384, 2048], P(('mp', 'expert'), 'seq'), may hold values from -0.046875 to 0.046875
- norm1_action: bfloat16 [1024], P('seq'), may hold values from 0.5 to 1.5
- query_action: bfloat16 [1024, 2048], P('seq', ('mp', 'expert')), may hold values from -0.1875 to 0.1875
- key_action: bfloat16 [1024, 256], P('seq'), may hold values from -0.1875 to 0.1875
- value_action: bfloat16 [1024, 256], P('seq'), may hold values from -0.1875 to 0.1875
- out_action: bfloat16 [2048, 1024], P(('mp', 'expert'), 'seq'), may hold values from -2 to 2
- norm2_action: bfloat16 [1024], P('seq'), may hold values from 0.5 to 1.5
- gate_action: bfloat16 [1024, 4096], P('seq', ('mp', 'expert')), may hold values from -0.1875 to 0.1875
- up_action: bfloat16 [1024, 4096], P('seq', ('mp', 'expert')), may hold values from -0.1875 to 0.1875
- down_action: bfloat16 [4096, 1024], P(('mp', 'expert'), 'seq'), may hold values from -0.09375 to 0.09375
- cot_prefix: bfloat16 [4480, 2048], P('seq'), may hold values from -6 to 6
- cot_action: bfloat16 [800, 1024], P('seq'), may hold values from -6 to 6
- instr_len: int32 [8], replicated, may hold values from 1 to 48, as said below
- slot_source: int32 [16], P('seq'), may hold values from -1 to 1, as said below
Outputs:
- y_prefix: bfloat16 [4480, 2048], P('seq')
- y_action: bfloat16 [800, 1024], P('seq')
- grad_hidden_prefix: float32 [4480, 2048], P('seq')
- grad_hidden_action: float32 [800, 1024], P('seq')
- grad_norm1_prefix: float32 [2048], P('seq')
- grad_query_prefix: float32 [2048, 2048], P('seq', ('mp', 'expert'))
- grad_key_prefix: float32 [2048, 256], P('seq')
- grad_value_prefix: float32 [2048, 256], P('seq')
- grad_out_prefix: float32 [2048, 2048], P(('mp', 'expert'), 'seq')
- grad_norm2_prefix: float32 [2048], P('seq')
- grad_gate_prefix: float32 [2048, 16384], P('seq', ('mp', 'expert'))
- grad_up_prefix: float32 [2048, 16384], P('seq', ('mp', 'expert'))
- grad_down_prefix: float32 [16384, 2048], P(('mp', 'expert'), 'seq')
- grad_norm1_action: float32 [1024], P('seq')
- grad_query_action: float32 [1024, 2048], P('seq', ('mp', 'expert'))
- grad_key_action: float32 [1024, 256], P('seq')
- grad_value_action: float32 [1024, 256], P('seq')
- grad_out_action: float32 [2048, 1024], P(('mp', 'expert'), 'seq')
- grad_norm2_action: float32 [1024], P('seq')
- grad_gate_action: float32 [1024, 4096], P('seq', ('mp', 'expert'))
- grad_up_action: float32 [1024, 4096], P('seq', ('mp', 'expert'))
- grad_down_action: float32 [4096, 1024], P(('mp', 'expert'), 'seq')
The draws below stay inside these ranges and needn't reach their ends.
Inputs may be any that keep to these rules, and one draw needn't show every extreme that they name: `instr_len`: each episode's instruction fills 1 to 48 of its slots; the rest of its prefix rows are padding. `slot_source`: each episode's action rows stand in exactly one slot: at its own seq index (0) or at the next seq index, cyclically (1); -1 marks an empty slot. A seq index holds 0 to 2 episodes. Episodes 0, 3, 6 and 7 always place theirs at the next seq index, episode 1 at its own.
All inputs are finite; a program needn't handle non-finite values.
Results may differ from the reference program's by a relative error of at most 0.015.
Values may be sent and summed in bfloat16 or wider, within the bound.
No kernel may reach another device: no remote copies, remote signals or barrier semaphores. Data moves between devices by JAX's collectives and lax.ppermute only.
A program may use at most 320 MiB of HBM per device.

```python
import jax
import jax.numpy as jnp
from jax import lax

DP = 2048
FFP = 16384
DA = 1024
FFA = 4096
H = 8
HD = 256
ACT = 50
IMG = 512
LANG = 48
SLOTS = 2
PREF = 560
EPISODES = 8


def draw_instr_len(key, part):
    key_len, key_pick = jax.random.split(jax.random.fold_in(key, 11))
    lengths = jax.random.randint(key_len, (EPISODES,), 1, LANG + 1)
    chosen = jax.random.randint(key_pick, (), 0, EPISODES)
    indices = jnp.arange(EPISODES)
    lengths = jnp.where(indices == chosen, LANG, lengths)
    lengths = jnp.where(indices == (chosen + 1) % EPISODES, 1, lengths)
    return lengths.astype(jnp.int32)


def draw_slot_source(key, part):
    key_step, key_place = jax.random.split(jax.random.fold_in(key, 23))
    steps_back = jax.random.randint(key_step, (EPISODES,), 0, 2)
    placing = jax.random.randint(key_place, (EPISODES,), 0, 2)
    indices = jnp.arange(EPISODES)
    moved = (indices == 0) | (indices == EPISODES - 2) | (indices == EPISODES - 1) | (indices == EPISODES // 2 - 1)
    stays = indices == 1
    steps_back = jnp.where(moved, 1, steps_back)
    steps_back = jnp.where(stays, 0, steps_back)
    before = jnp.roll(steps_back, 1)
    own_slot = jnp.where(steps_back == 0, 0, -1)
    moved_slot = jnp.where(before == 1, 1, -1)
    first_slot = jnp.where(placing == 0, own_slot, moved_slot)
    second_slot = jnp.where(placing == 0, moved_slot, own_slot)
    return jnp.stack([first_slot, second_slot], axis=1).reshape(EPISODES * SLOTS).astype(jnp.int32)


def level_of(rng, shape, pieces, least, largest):
    factor_of, own = 1.0, jax.random.fold_in(rng, 6)
    for axis_at, parts in pieces:
        steps = jnp.exp(jax.random.uniform(jax.random.fold_in(own, axis_at), (parts,), jnp.float32, least / len(pieces), largest / len(pieces)))
        factor_of = factor_of * jnp.repeat(steps, shape[axis_at] // parts).reshape([-1 if axis == axis_at else 1 for axis in range(len(shape))])
    return factor_of


def noise(rng, dims, deviation, reach, cuts=(), kind=jnp.bfloat16):
    entries = deviation * jax.random.normal(rng, dims, jnp.float32)
    if cuts:
        entries = entries * level_of(rng, dims, cuts, -0.22, 0.18)
    return jnp.clip(entries, -reach, reach).astype(kind)


def setup_inputs(seed: int = 0) -> dict:
    keys = jax.random.split(jax.random.key(seed), 25)
    return {
        "hidden_prefix": noise(keys[0], (EPISODES * PREF, DP), 1.0, 6.0, ((0, 8),)),
        "hidden_action": noise(keys[1], (EPISODES * SLOTS * ACT, DA), 1.0, 6.0, ((0, 8),)),
        "norm1_prefix": jnp.clip(1.0 + 0.1 * jax.random.normal(keys[2], (DP,), jnp.float32), 0.5, 1.5).astype(jnp.bfloat16),
        "query_prefix": noise(keys[3], (DP, H * HD), DP ** -0.5, 0.125, ((0, 8), (1, 4))),
        "key_prefix": noise(keys[4], (DP, HD), DP ** -0.5, 0.125, ((0, 8),)),
        "value_prefix": noise(keys[5], (DP, HD), DP ** -0.5, 0.125, ((0, 8),)),
        "out_prefix": noise(keys[6], (H * HD, DP), (max(2, H * HD * 3 // PREF)) ** -0.5, 2.0, ((0, 4), (1, 8))),
        "norm2_prefix": jnp.clip(1.0 + 0.1 * jax.random.normal(keys[7], (DP,), jnp.float32), 0.5, 1.5).astype(jnp.bfloat16),
        "gate_prefix": noise(keys[8], (DP, FFP), DP ** -0.5, 0.125, ((0, 8), (1, 4))),
        "up_prefix": noise(keys[9], (DP, FFP), DP ** -0.5, 0.125, ((0, 8), (1, 4))),
        "down_prefix": noise(keys[10], (FFP, DP), FFP ** -0.5, 0.046875, ((0, 4), (1, 8))),
        "norm1_action": jnp.clip(1.0 + 0.1 * jax.random.normal(keys[11], (DA,), jnp.float32), 0.5, 1.5).astype(jnp.bfloat16),
        "query_action": noise(keys[12], (DA, H * HD), DA ** -0.5, 0.1875, ((0, 8), (1, 4))),
        "key_action": noise(keys[13], (DA, HD), DA ** -0.5, 0.1875, ((0, 8),)),
        "value_action": noise(keys[14], (DA, HD), DA ** -0.5, 0.1875, ((0, 8),)),
        "out_action": noise(keys[15], (H * HD, DA), (max(2, H * HD * 3 // (PREF + ACT))) ** -0.5, 2.0, ((0, 4), (1, 8))),
        "norm2_action": jnp.clip(1.0 + 0.1 * jax.random.normal(keys[16], (DA,), jnp.float32), 0.5, 1.5).astype(jnp.bfloat16),
        "gate_action": noise(keys[17], (DA, FFA), DA ** -0.5, 0.1875, ((0, 8), (1, 4))),
        "up_action": noise(keys[18], (DA, FFA), DA ** -0.5, 0.1875, ((0, 8), (1, 4))),
        "down_action": noise(keys[19], (FFA, DA), FFA ** -0.5, 0.09375, ((0, 4), (1, 8))),
        "cot_prefix": noise(keys[20], (EPISODES * PREF, DP), 1.0, 6.0, ((0, 8),)),
        "cot_action": noise(keys[21], (EPISODES * SLOTS * ACT, DA), 1.0, 6.0, ((0, 8),)),
        "instr_len": draw_instr_len(jax.random.fold_in(keys[24], 71), 0),
        "slot_source": draw_slot_source(jax.random.fold_in(keys[24], 71), 0),
    }


EPS = 1e-06
MASKED = -1e+30

@jax.custom_vjp
def low(v):
    return lax.optimization_barrier(v.astype(jnp.bfloat16)).astype(jnp.float32)

@jax.custom_vjp
def low_back(v):
    return v

def low_keep(v):
    return (low(v), None)

def low_pass(kept, grad):
    return (grad,)

def back_keep(v):
    return (v, None)

def back_low(kept, grad):
    return (low(grad),)
low.defvjp(low_keep, low_pass)
low_back.defvjp(back_keep, back_low)

def matmul(left_op, right_op):
    return jnp.dot(left_op, right_op, precision=lax.Precision.HIGHEST)

def rms_norm(values, gain_vec):
    return values * lax.rsqrt(lax.optimization_barrier(jnp.mean(values * values, axis=-1, keepdims=True)) + EPS) * gain_vec

def attend(query_flat, key_rows, value_rows, keep_mask):
    row_count = query_flat.shape[0]
    query_heads = query_flat.reshape(row_count, H, HD)
    scores = jnp.einsum('qhd,kd->hqk', query_heads, key_rows, precision=lax.Precision.HIGHEST) * HD ** (-0.5)
    scores = low_back(scores)
    scores = jnp.where(keep_mask[None, None, :], scores, MASKED)
    prob_low = low(jax.nn.softmax(scores, axis=-1))
    mixed_rows = jnp.einsum('hqk,kd->qhd', prob_low, value_rows, precision=lax.Precision.HIGHEST)
    return low(low_back(mixed_rows.reshape(row_count, H * HD)))

def project(weights, hidden_rows):
    normed = low(rms_norm(hidden_rows, weights[0]))
    query_rows = low(low_back(matmul(normed, weights[1])))
    key_rows = low(low_back(matmul(normed, weights[2])))
    value_rows = low(low_back(matmul(normed, weights[3])))
    return (query_rows, key_rows, value_rows)

def finish(weights, hidden_rows, mixed_rows, live_gain):
    attn_rows = low_back(matmul(mixed_rows, weights[4])) * live_gain
    middle = hidden_rows + attn_rows
    normed = low(rms_norm(middle, weights[5]))
    gate_pre = low_back(matmul(normed, weights[6]))
    up_pre = low_back(matmul(normed, weights[7]))
    hidden_mid = low(jax.nn.gelu(gate_pre, approximate=True) * up_pre)
    return middle + low_back(matmul(hidden_mid, weights[8])) * live_gain

def forward(weights_p, weights_a, x_pre, x_act, lengths, sources):
    positions = jnp.arange(PREF, dtype=jnp.int32)

    def one_prefix(carry_in):
        hidden_rows, length = carry_in
        query_rows, key_rows, value_rows = project(weights_p, hidden_rows)
        keep_mask = positions < IMG + length
        mixed_rows = attend(query_rows, key_rows, value_rows, keep_mask)
        return (finish(weights_p, hidden_rows, mixed_rows, 1.0), key_rows, value_rows)
    out_pre, keys_all, values_all = lax.map(jax.checkpoint(one_prefix), (x_pre, lengths))

    def one_dest(carry_in):
        hidden_slots, source_row, dest_index = carry_in

        def one_slot(hidden_rows, source):
            live_flag = source >= 0
            offset = jnp.where(live_flag, source, 0).astype(jnp.int32)
            episode = (dest_index - offset + EPISODES) % EPISODES
            keep_pre = (positions < IMG + lengths[episode]) & live_flag
            query_rows, key_rows, value_rows = project(weights_a, hidden_rows)
            key_cat = jnp.concatenate([keys_all[episode], key_rows], axis=0)
            value_cat = jnp.concatenate([values_all[episode], value_rows], axis=0)
            keep_mask = jnp.concatenate([keep_pre, jnp.ones((ACT,), dtype=bool)])
            mixed_rows = attend(query_rows, key_cat, value_cat, keep_mask)
            return finish(weights_a, hidden_rows, mixed_rows, live_flag.astype(jnp.float32))
        return jax.vmap(one_slot)(hidden_slots, source_row)
    dest_all = jnp.arange(EPISODES, dtype=jnp.int32)
    out_act = lax.map(jax.checkpoint(one_dest), (x_act, sources, dest_all))
    return (out_pre, out_act)

def reference(hidden_prefix, hidden_action, norm1_prefix, query_prefix, key_prefix, value_prefix, out_prefix, norm2_prefix, gate_prefix, up_prefix, down_prefix, norm1_action, query_action, key_action, value_action, out_action, norm2_action, gate_action, up_action, down_action, cot_prefix, cot_action, instr_len, slot_source):
    weights_p = tuple((weight_item.astype(jnp.float32) for weight_item in (norm1_prefix, query_prefix, key_prefix, value_prefix, out_prefix, norm2_prefix, gate_prefix, up_prefix, down_prefix)))
    weights_a = tuple((weight_item.astype(jnp.float32) for weight_item in (norm1_action, query_action, key_action, value_action, out_action, norm2_action, gate_action, up_action, down_action)))
    x_pre = hidden_prefix.astype(jnp.float32).reshape(EPISODES, PREF, DP)
    x_act = hidden_action.astype(jnp.float32).reshape(EPISODES, SLOTS, ACT, DA)
    sources = slot_source.reshape(EPISODES, SLOTS)

    def run_layer(w_pre, w_act, in_pre, in_act):
        return forward(w_pre, w_act, in_pre, in_act, instr_len, sources)
    (out_pre, out_act), pullback = jax.vjp(run_layer, weights_p, weights_a, x_pre, x_act)
    cot_pre = cot_prefix.astype(jnp.float32).reshape(EPISODES, PREF, DP)
    cot_act = cot_action.astype(jnp.float32).reshape(EPISODES, SLOTS, ACT, DA)
    grad_w_pre, grad_w_act, grad_pre, grad_act = pullback((cot_pre, cot_act))
    return (out_pre.reshape(EPISODES * PREF, DP).astype(jnp.bfloat16), out_act.reshape(EPISODES * SLOTS * ACT, DA).astype(jnp.bfloat16), grad_pre.reshape(EPISODES * PREF, DP), grad_act.reshape(EPISODES * SLOTS * ACT, DA), grad_w_pre[0], grad_w_pre[1], grad_w_pre[2], grad_w_pre[3], grad_w_pre[4], grad_w_pre[5], grad_w_pre[6], grad_w_pre[7], grad_w_pre[8], grad_w_act[0], grad_w_act[1], grad_w_act[2], grad_w_act[3], grad_w_act[4], grad_w_act[5], grad_w_act[6], grad_w_act[7], grad_w_act[8])
```

```python
import jax
import jax.numpy as jnp
from jax import lax
from jax.sharding import PartitionSpec as P

IMG = 512
EPS = 1e-06
MASKED = -1e30
BF = jnp.bfloat16
F32 = jnp.float32

SNAKE = (0, 2, 4, 6, 7, 5, 3, 1)


def dot(left, right, left_dim, right_dim):
    return lax.dot_general(
        left, right, (((left_dim,), (right_dim,)), ((), ())), preferred_element_type=F32
    )


def cat(parts, axis=0):
    return parts[0] if len(parts) == 1 else jnp.concatenate(parts, axis=axis)


def pad_rows(block, rows):
    missing = rows - block.shape[0]
    return jnp.pad(block, ((0, missing), (0, 0))) if missing else block


def shift(block, axis, distance):
    count = lax.axis_size(axis)
    return lax.ppermute(block, axis, [(i, (i + distance) % count) for i in range(count)])


def ring_step(block, step):
    pairs = [(SNAKE[i], SNAKE[(i + step) % len(SNAKE)]) for i in range(len(SNAKE))]
    return lax.ppermute(block, "seq", pairs)


def on_ring():
    return lax.axis_size("seq") == len(SNAKE)


def seq_gather(block):
    if not on_ring():
        return [lax.all_gather(block, "seq", axis=0, tiled=True)]
    count = len(SNAKE)
    ahead, behind = [block], [block]
    for _ in range(count // 2):
        ahead.append(ring_step(ahead[-1], -1))
    for _ in range((count - 1) // 2):
        behind.append(ring_step(behind[-1], 1))
    return [cat([behind[k], ahead[k + 1]]) for k in range(count // 2)]


def seq_reduce(groups):
    if not on_ring():
        return lax.psum_scatter(
            groups[0].astype(BF), "seq", scatter_dimension=0, tiled=True
        ).astype(F32)
    half = groups[0].shape[0] // 2
    top = len(groups)
    going = groups[top - 1][half:].astype(BF)
    back = groups[top - 1][:half].astype(BF)
    for k in range(top - 2, -1, -1):
        going = ring_step(going, 1).astype(F32) + groups[k][half:].astype(F32)
        going = going.astype(BF)
        back = ring_step(back, -1).astype(F32) + groups[k][:half].astype(F32)
        if k:
            back = back.astype(BF)
    return back + ring_step(going, 1).astype(F32)


def swap(block, axis):
    return shift(block, axis, 1)


def quad_gather_rel(block):
    across = swap(block, "mp")
    other = swap(jnp.stack([block, across]), "expert")
    return [block, across, other[0], other[1]]


def quad_gather(block):
    m, e = lax.axis_index("mp"), lax.axis_index("expert")
    across = swap(block, "mp")
    mine = jnp.where(m == 0, jnp.stack([block, across]), jnp.stack([across, block]))
    other = swap(mine, "expert")
    both = jnp.where(e == 0, jnp.stack([mine, other], 1), jnp.stack([other, mine], 1))
    return both.reshape((4,) + block.shape)


def quad_reduce(whole):
    m, e = lax.axis_index("mp"), lax.axis_index("expert")
    parts = whole.reshape((2, 2) + whole.shape[1:])
    give = lax.dynamic_index_in_dim(parts, 1 - e, 1, keepdims=False).astype(BF)
    keep = lax.dynamic_index_in_dim(parts, e, 1, keepdims=False).astype(F32)
    pair = keep + swap(give, "expert").astype(F32)
    give = lax.dynamic_index_in_dim(pair, 1 - m, 0, keepdims=False).astype(BF)
    keep = lax.dynamic_index_in_dim(pair, m, 0, keepdims=False)
    return keep + swap(give, "mp").astype(F32)


def quad_reduce_rel(whole):
    parts = whole.reshape((2, 2) + (whole.shape[0] // 4,) + whole.shape[1:])
    pair = parts[0].astype(F32) + swap(parts[1].astype(BF), "expert").astype(F32)
    return (pair[0] + swap(pair[1].astype(BF), "mp").astype(F32)).astype(BF)


def hidden_first(weight, from_rows):
    count = lax.axis_size("seq")
    if from_rows:
        depth, width = weight.shape
        parts = weight.reshape(depth, count, width // count).transpose(1, 2, 0)
    else:
        width, depth = weight.shape
        parts = weight.reshape(count, width // count, depth)
    parts = lax.all_to_all(parts, "seq", 0, 0, tiled=True)
    return parts.transpose(1, 0, 2).reshape(width // count, count * depth)


def hidden_back(grad, to_rows):
    count = lax.axis_size("seq")
    width, full = grad.shape
    depth = full // count
    parts = grad.reshape(width, count, depth).transpose(1, 0, 2)
    parts = lax.all_to_all(parts, "seq", 0, 0, tiled=True)
    if to_rows:
        return parts.transpose(2, 0, 1).reshape(depth, count * width).astype(F32)
    return parts.reshape(count * width, depth).astype(F32)


def spread(weight, from_rows):
    return cat(quad_gather_rel(hidden_first(weight, from_rows)))


def collect(grad, to_rows):
    return hidden_back(quad_reduce_rel(grad), to_rows)


def rms_norm(values, gain_vec):
    return values * lax.rsqrt(jnp.mean(values * values, axis=-1, keepdims=True) + EPS) * gain_vec


def norm_backward(values, gain_vec, grad_normed):
    return jax.vjp(rms_norm, values, gain_vec)[1](grad_normed)


def geglu_act(gate_pre, up_pre):
    return jax.nn.gelu(gate_pre, approximate=True) * up_pre


def attend_forward(query_flat, key_rows, value_rows, keep_mask):
    row_count = query_flat.shape[0]
    head_size = key_rows.shape[1]
    query_heads = query_flat.reshape(row_count, -1, head_size)
    scores = jnp.einsum(
        "qhd,kd->hqk", query_heads, key_rows, preferred_element_type=F32
    ) * (head_size ** (-0.5))
    scores = jnp.where(keep_mask[None, None, :], scores, MASKED)
    expo = jnp.exp(scores - jnp.max(scores, axis=-1, keepdims=True))
    probs = expo / jnp.sum(expo, axis=-1, keepdims=True)
    mixed_rows = jnp.einsum(
        "hqk,kd->qhd", probs.astype(BF), value_rows, preferred_element_type=F32
    )
    return mixed_rows.reshape(row_count, -1).astype(BF), probs


def attend_backward(query_flat, key_rows, value_rows, probs, grad_mixed):
    row_count = query_flat.shape[0]
    head_size = key_rows.shape[1]
    score_scale = head_size ** (-0.5)
    query_heads = query_flat.reshape(row_count, -1, head_size)
    grad_heads = grad_mixed.reshape(row_count, -1, head_size)
    grad_probs = jnp.einsum("qhd,kd->hqk", grad_heads, value_rows, preferred_element_type=F32)
    row_inner = jnp.sum(grad_probs * probs, axis=-1, keepdims=True)
    grad_scores = (probs * (grad_probs - row_inner)).astype(BF)
    grad_query = jnp.einsum("hqk,kd->qhd", grad_scores, key_rows, preferred_element_type=F32)
    grad_query = (grad_query * score_scale).reshape(row_count, -1).astype(BF)
    grad_keys = score_scale * jnp.einsum(
        "hqk,qhd->kd", grad_scores, query_heads, preferred_element_type=F32
    )
    grad_values = jnp.einsum(
        "hqk,qhd->kd", probs.astype(BF), grad_heads, preferred_element_type=F32
    )
    return grad_query, jnp.concatenate([grad_keys, grad_values], axis=1)


def feed_forward(normed_groups, cot_groups, w_gate, w_up, w_down):
    y_groups, gn_groups, mids, d_gates, d_ups = [], [], [], [], []
    for normed, cot in zip(normed_groups, cot_groups):
        gate_pre = dot(normed, w_gate, 1, 1)
        up_pre = dot(normed, w_up, 1, 1)
        grad_hidden = dot(cot, w_down, 1, 1)
        mid, pullback = jax.vjp(geglu_act, gate_pre, up_pre)
        d_gate, d_up = pullback(grad_hidden)
        mid, d_gate, d_up = mid.astype(BF), d_gate.astype(BF), d_up.astype(BF)
        gn_groups.append((dot(d_gate, w_gate, 1, 0) + dot(d_up, w_up, 1, 0)).astype(BF))
        y_groups.append(dot(mid, w_down, 1, 0).astype(BF))
        mids.append(mid)
        d_gates.append(d_gate)
        d_ups.append(d_up)
    return y_groups, gn_groups, cat(mids), cat(d_gates), cat(d_ups)


def weight_grad(left, right):
    return dot(left, right, 0, 0).astype(BF)


def body(
    hidden_prefix,
    hidden_action,
    norm1_prefix,
    query_prefix,
    key_prefix,
    value_prefix,
    out_prefix,
    norm2_prefix,
    gate_prefix,
    up_prefix,
    down_prefix,
    norm1_action,
    query_action,
    key_action,
    value_action,
    out_action,
    norm2_action,
    gate_action,
    up_action,
    down_action,
    cot_prefix,
    cot_action,
    instr_len,
    slot_source,
):
    seq_index = lax.axis_index("seq")
    episodes = lax.axis_size("seq")
    quad = lax.axis_size("mp") * lax.axis_size("expert")
    mine = lax.axis_index("mp") * lax.axis_size("expert") + lax.axis_index("expert")
    prefix_rows, action_rows_all = hidden_prefix.shape[0], hidden_action.shape[0]
    slot_count = slot_source.shape[0]
    action_rows = action_rows_all // slot_count
    head_size = key_prefix.shape[1]
    head_cols = query_prefix.shape[1]
    part_p = -(-prefix_rows // (16 * quad)) * 16
    part_a = -(-action_rows_all // (16 * quad)) * 16
    kv_cols = 2 * head_size // quad

    def quarter_kv(w_key, w_value):
        return lax.dynamic_slice_in_dim(
            jnp.concatenate([w_key, w_value], axis=1), mine * kv_cols, kv_cols, axis=1
        )

    early_cols = head_cols + kv_cols
    depth_p, depth_a = query_prefix.shape[0], query_action.shape[0]
    gains = jnp.concatenate([norm1_prefix, norm2_prefix, norm1_action, norm2_action])
    gain_rows = -(-gains.shape[0] // (16 * early_cols)) * 16
    gain_block = jnp.pad(gains, (0, gain_rows * early_cols - gains.shape[0]))
    early = jnp.concatenate(
        [
            jnp.concatenate([query_prefix, quarter_kv(key_prefix, value_prefix)], axis=1),
            jnp.concatenate([query_action, quarter_kv(key_action, value_action)], axis=1),
            gain_block.reshape(gain_rows, early_cols),
        ],
        axis=0,
    )
    early = lax.all_gather(early, "seq", axis=0, tiled=False)
    w_in_p = early[:, :depth_p].reshape(-1, early_cols)
    w_in_a = early[:, depth_p : depth_p + depth_a].reshape(-1, early_cols)
    gains = early[:, depth_p + depth_a :].reshape(episodes, -1)
    gain1_p = gains[:, :depth_p].reshape(-1).astype(F32)
    gain2_p = gains[:, depth_p : 2 * depth_p].reshape(-1).astype(F32)
    gain1_a = gains[:, 2 * depth_p : 2 * depth_p + depth_a].reshape(-1).astype(F32)
    gain2_a = gains[:, 2 * depth_p + depth_a : 2 * (depth_p + depth_a)].reshape(-1).astype(F32)

    w_gate_p, w_up_p = spread(gate_prefix, True), spread(up_prefix, True)
    w_gate_a, w_up_a = spread(gate_action, True), spread(up_action, True)
    late = jnp.concatenate([out_prefix, out_action], axis=1)
    late = lax.all_gather(late, "seq", axis=0, tiled=False)
    w_out_p = late[:, :, :depth_p].transpose(1, 0, 2).reshape(head_cols, -1)
    w_out_a = late[:, :, depth_p:].transpose(1, 0, 2).reshape(head_cols, -1)
    w_down_p, w_down_a = spread(down_prefix, False), spread(down_action, False)

    positions = jnp.arange(prefix_rows, dtype=jnp.int32)
    keep_prefix = positions < IMG + instr_len[seq_index]
    live_slot = slot_source >= 0
    offsets = jnp.where(live_slot, slot_source, 0)
    source_ep = (seq_index - offsets + episodes) % episodes
    keep_slots = (positions[None, :] < IMG + instr_len[source_ep][:, None]) & live_slot[:, None]
    keep_all = jnp.concatenate(
        [keep_slots, jnp.ones((slot_count, action_rows), dtype=bool)], axis=1
    )
    from_prev = slot_source == 1
    from_here = slot_source == 0
    live_rows = jnp.repeat(live_slot.astype(F32), action_rows)[:, None]

    def own_part(rows, part):
        return lax.dynamic_slice_in_dim(pad_rows(rows, quad * part), mine * part, part, axis=0)

    x_p, x_a = own_part(hidden_prefix, part_p), own_part(hidden_action, part_a)
    x_p, x_a = x_p.astype(F32), x_a.astype(F32)
    live_a = own_part(live_rows, part_a)
    cot_p, cot_a = own_part(cot_prefix, part_p), own_part(cot_action, part_a)
    cot_full_p = seq_gather(cot_p)
    cot_full_a = seq_gather((cot_a.astype(F32) * live_a).astype(BF))

    normed1_p = rms_norm(hidden_prefix.astype(F32), gain1_p).astype(BF)
    normed1_a = rms_norm(hidden_action.astype(F32), gain1_a).astype(BF)
    in_p, in_a = dot(normed1_p, w_in_p, 1, 0).astype(BF), dot(normed1_a, w_in_a, 1, 0).astype(BF)
    query_p, query_a = in_p[:, :head_cols], in_a[:, :head_cols]
    kv_both = quad_gather(jnp.concatenate([in_p[:, head_cols:], in_a[:, head_cols:]], axis=0))
    kv_both = kv_both.transpose(1, 0, 2).reshape(-1, 2 * head_size)
    kv_p, kv_a = kv_both[:prefix_rows], kv_both[prefix_rows:]
    kv_prev = shift(kv_p, "seq", 1)
    keys_p, values_p = kv_p[:, :head_size], kv_p[:, head_size:]
    mixed_p, probs_p = attend_forward(query_p, keys_p, values_p, keep_prefix)
    kv_slots = jnp.where(from_prev[:, None, None], kv_prev[None], kv_p[None])
    kv_slots = jnp.concatenate([kv_slots, kv_a.reshape(slot_count, action_rows, -1)], axis=1)
    keys_slots, values_slots = kv_slots[:, :, :head_size], kv_slots[:, :, head_size:]
    query_slots = query_a.reshape(slot_count, action_rows, -1)
    mixed_slots, probs_a = jax.vmap(attend_forward)(
        query_slots, keys_slots, values_slots, keep_all
    )
    mixed_a = mixed_slots.reshape(action_rows_all, -1)
    attn_p = dot(pad_rows(mixed_p, quad * part_p), w_out_p, 1, 0)
    attn_a = dot(pad_rows(mixed_a, quad * part_a), w_out_a, 1, 0)
    middle_p = x_p + quad_reduce(attn_p.reshape(quad, part_p, -1))
    middle_a = x_a + live_a * quad_reduce(attn_a.reshape(quad, part_a, -1))

    normed2_p = seq_gather(rms_norm(middle_p, gain2_p).astype(BF))
    normed2_a = seq_gather(rms_norm(middle_a, gain2_a).astype(BF))
    y_p, gn2_p, mid_p, d_gate_p, d_up_p = feed_forward(
        normed2_p, cot_full_p, w_gate_p, w_up_p, w_down_p
    )
    y_a, gn2_a, mid_a, d_gate_a, d_up_a = feed_forward(
        normed2_a, cot_full_a, w_gate_a, w_up_a, w_down_a
    )
    gn2_p, gn2_a = seq_reduce(gn2_p), seq_reduce(gn2_a)
    normed2_p, normed2_a = cat(normed2_p), cat(normed2_a)
    cot_full_p, cot_full_a = cat(cot_full_p), cat(cot_full_a)
    y_p = (middle_p + seq_reduce(y_p)).astype(BF)
    y_a = (middle_a + live_a * seq_reduce(y_a)).astype(BF)

    dmid_norm_p, dgain2_p = norm_backward(middle_p, gain2_p, gn2_p)
    dmid_norm_a, dgain2_a = norm_backward(middle_a, gain2_a, gn2_a)
    dmid_p = cot_p.astype(F32) + dmid_norm_p
    dmid_a = cot_a.astype(F32) + dmid_norm_a
    dao_p = quad_gather(dmid_p.astype(BF)).reshape(quad * part_p, -1)[:prefix_rows]
    dao_a = quad_gather((dmid_a * live_a).astype(BF)).reshape(quad * part_a, -1)
    dao_a = dao_a[:action_rows_all]

    dmix_p, dmix_a = dot(dao_p, w_out_p, 1, 1).astype(BF), dot(dao_a, w_out_a, 1, 1).astype(BF)
    dq_slots, dkv_slots = jax.vmap(attend_backward)(
        query_slots,
        keys_slots,
        values_slots,
        probs_a,
        dmix_a.reshape(slot_count, action_rows, -1),
    )
    dkv_pre = dkv_slots[:, :prefix_rows]
    dkv_a = dkv_slots[:, prefix_rows:].reshape(action_rows_all, -1)
    to_prev = jnp.sum(jnp.where(from_prev[:, None, None], dkv_pre, 0.0), axis=0)
    to_here = jnp.sum(jnp.where(from_here[:, None, None], dkv_pre, 0.0), axis=0)
    returned = shift(to_prev.astype(BF), "seq", -1).astype(F32)
    dq_p, dkv_p = attend_backward(query_p, keys_p, values_p, probs_p, dmix_p)
    dkv_p = dkv_p + to_here + returned
    dq_a = dq_slots.reshape(action_rows_all, -1)

    dkv_both = jnp.concatenate([dkv_p, dkv_a], axis=0)
    dkv_both = dkv_both.reshape(-1, quad, kv_cols).transpose(1, 0, 2)
    dkv_both = quad_reduce(dkv_both).astype(BF)
    din_p = jnp.concatenate([dq_p, dkv_both[:prefix_rows]], axis=1)
    din_a = jnp.concatenate([dq_a, dkv_both[prefix_rows:]], axis=1)
    gn1_p = dot(pad_rows(din_p, quad * part_p), w_in_p, 1, 1)
    gn1_a = dot(pad_rows(din_a, quad * part_a), w_in_a, 1, 1)
    gn1_p = quad_reduce(gn1_p.reshape(quad, part_p, -1))
    gn1_a = quad_reduce(gn1_a.reshape(quad, part_a, -1))
    dx_norm_p, dgain1_p = norm_backward(x_p, gain1_p, gn1_p)
    dx_norm_a, dgain1_a = norm_backward(x_a, gain1_a, gn1_a)
    dx_p = quad_gather((dmid_p + dx_norm_p).astype(BF)).reshape(quad * part_p, -1)
    dx_a = quad_gather((dmid_a + dx_norm_a).astype(BF)).reshape(quad * part_a, -1)
    dx_p = dx_p[:prefix_rows].astype(F32)
    dx_a = dx_a[:action_rows_all].astype(F32)
    y_p = quad_gather(y_p).reshape(quad * part_p, -1)[:prefix_rows]
    y_a = quad_gather(y_a).reshape(quad * part_a, -1)[:action_rows_all]

    dwd_p = collect(weight_grad(mid_p, cot_full_p), False)
    dwd_a = collect(weight_grad(mid_a, cot_full_a), False)
    dwg_p = collect(weight_grad(d_gate_p, normed2_p), True)
    dwg_a = collect(weight_grad(d_gate_a, normed2_a), True)
    dwu_p = collect(weight_grad(d_up_p, normed2_p), True)
    dwu_a = collect(weight_grad(d_up_a, normed2_a), True)

    dwo = jnp.concatenate(
        [
            weight_grad(mixed_p, dao_p).reshape(head_cols, episodes, -1),
            weight_grad(mixed_a, dao_a).reshape(head_cols, episodes, -1),
        ],
        axis=2,
    ).transpose(1, 0, 2)
    dwo = lax.psum_scatter(dwo, "seq", scatter_dimension=0, tiled=False).astype(F32)
    dw_in = jnp.concatenate(
        [
            weight_grad(normed1_p, din_p).reshape(episodes, -1, early_cols),
            weight_grad(normed1_a, din_a).reshape(episodes, -1, early_cols),
        ],
        axis=1,
    )
    dw_in = lax.psum_scatter(dw_in, "seq", scatter_dimension=0, tiled=False)
    dw_kv = quad_gather(dw_in[:, head_cols:]).transpose(1, 0, 2).reshape(-1, 2 * head_size)
    dw_kv = dw_kv.astype(F32)
    dw_in = dw_in.astype(F32)

    dgains = jnp.concatenate(
        [g.reshape(episodes, -1) for g in (dgain1_p, dgain2_p, dgain1_a, dgain2_a)], axis=1
    )
    dgains = lax.psum_scatter(dgains, "seq", scatter_dimension=0, tiled=False)
    dgains = lax.psum(dgains, ("mp", "expert"))
    return (
        y_p,
        y_a,
        dx_p,
        dx_a,
        dgains[:depth_p],
        dw_in[:depth_p, :head_cols],
        dw_kv[:depth_p, :head_size],
        dw_kv[:depth_p, head_size:],
        dwo[:, :depth_p],
        dgains[depth_p : 2 * depth_p],
        dwg_p,
        dwu_p,
        dwd_p,
        dgains[2 * depth_p : 2 * depth_p + depth_a],
        dw_in[depth_p:, :head_cols],
        dw_kv[depth_p:, :head_size],
        dw_kv[depth_p:, head_size:],
        dwo[:, depth_p:],
        dgains[2 * depth_p + depth_a :],
        dwg_a,
        dwu_a,
        dwd_a,
    )


def solution(mesh):
    rows, flat = P("seq", None), P("seq")
    wide, tall = P("seq", ("mp", "expert")), P(("mp", "expert"), "seq")
    one_expert = (flat, wide, rows, rows, tall, flat, wide, wide, tall)
    return jax.shard_map(
        body,
        mesh=mesh,
        in_specs=(rows, rows) + one_expert + one_expert + (rows, rows, P(), flat),
        out_specs=(rows, rows, rows, rows) + one_expert + one_expert,
        check_vma=False,
    )
```

```python
import jax
import jax.numpy as jnp
from jax import lax
from jax.sharding import PartitionSpec as P

IMG = 512
LANES = 128
EPS = 1e-06
MASKED = -1e30
BF = jnp.bfloat16
F32 = jnp.float32

SNAKE = (0, 2, 4, 6, 7, 5, 3, 1)


def dot(left, right, left_dim, right_dim):
    return lax.dot_general(
        left, right, (((left_dim,), (right_dim,)), ((), ())), preferred_element_type=F32
    )


def fence(*values):
    return lax.optimization_barrier(values)


def fold(block, width):
    return cat([block[:, k : k + width] for k in range(0, block.shape[1], width)])


def unfold(block, rows):
    return cat([block[..., k : k + rows, :] for k in range(0, block.shape[-2], rows)], -1)


def cat(parts, axis=0):
    return parts[0] if len(parts) == 1 else jnp.concatenate(parts, axis=axis)


def pad_rows(block, rows):
    missing = rows - block.shape[0]
    return jnp.pad(block, ((0, missing), (0, 0))) if missing else block


def shift(block, axis, distance):
    count = lax.axis_size(axis)
    return lax.ppermute(block, axis, [(i, (i + distance) % count) for i in range(count)])


def ring_step(block, step):
    pairs = [(SNAKE[i], SNAKE[(i + step) % len(SNAKE)]) for i in range(len(SNAKE))]
    return lax.ppermute(block, "seq", pairs)


def on_ring():
    return lax.axis_size("seq") == len(SNAKE)


def ring_gather(block):
    ahead, behind, order = [block], [block], [block]
    for k in range(1, len(SNAKE)):
        if k % 2:
            ahead.append(ring_step(ahead[-1], -1))
            order.append(ahead[-1])
        else:
            behind.append(ring_step(behind[-1], 1))
            order.append(behind[-1])
    return order


def seq_gather(block):
    if on_ring():
        return ring_gather(block)
    whole = lax.all_gather(block, "seq", axis=0, tiled=False)
    return [whole[k] for k in range(whole.shape[0])]


def seq_reduce(blocks):
    if not on_ring():
        return lax.psum_scatter(jnp.stack(blocks), "seq", scatter_dimension=0).astype(F32)
    going, back = blocks[-1], blocks[-2]
    for k in range(len(blocks) - 3, 0, -2):
        going = (ring_step(going, 1).astype(F32) + blocks[k].astype(F32)).astype(BF)
        back = ring_step(back, -1).astype(F32) + blocks[k - 1].astype(F32)
        if k > 1:
            back = back.astype(BF)
    return back + ring_step(going, 1).astype(F32)


def seq_halve(rows):
    count, index = rows.shape[0], lax.axis_index("seq")
    while count > 1:
        count //= 2
        bit = (index // count) % 2
        halves = rows.reshape(2, count, -1)
        keep = lax.dynamic_index_in_dim(halves, bit, 0, keepdims=False)
        give = lax.dynamic_index_in_dim(halves, 1 - bit, 0, keepdims=False)
        pairs = [(i, i ^ count) for i in range(lax.axis_size("seq"))]
        rows = keep + lax.ppermute(give, "seq", pairs)
    rows = rows + shift(rows, "expert", 1)
    return (rows + shift(rows, "mp", 1)).reshape(-1)


def swap(block, axis):
    return shift(block, axis, 1)


def quad_join(block, across, axis):
    return cat([block, across, swap(block, "expert"), swap(across, "expert")], axis)


def quad_gather(block):
    m, e = lax.axis_index("mp"), lax.axis_index("expert")
    across = swap(block, "mp")
    mine = jnp.where(m == 0, jnp.stack([block, across]), jnp.stack([across, block]))
    other = swap(mine, "expert")
    both = jnp.where(e == 0, jnp.stack([mine, other], 1), jnp.stack([other, mine], 1))
    return both.reshape((4,) + block.shape)


def quad_reduce(whole):
    m, e = lax.axis_index("mp"), lax.axis_index("expert")
    parts = whole.reshape((2, 2) + whole.shape[1:])
    give = lax.dynamic_index_in_dim(parts, 1 - e, 1, keepdims=False).astype(BF)
    keep = lax.dynamic_index_in_dim(parts, e, 1, keepdims=False).astype(F32)
    pair = keep + swap(give, "expert").astype(F32)
    give = lax.dynamic_index_in_dim(pair, 1 - m, 0, keepdims=False).astype(BF)
    keep = lax.dynamic_index_in_dim(pair, m, 0, keepdims=False)
    return keep + swap(give, "mp").astype(F32)


def quad_reduce_rel(parts):
    give = parts[1].astype(F32) + swap(parts[3].astype(BF), "expert").astype(F32)
    keep = parts[0].astype(F32) + swap(parts[2].astype(BF), "expert").astype(F32)
    return (keep + swap(give.astype(BF), "mp").astype(F32)).astype(BF)


def pack(prefix, action):
    fold = prefix.shape[-1] // action.shape[-1]
    rows = action.shape[-2] // fold
    parts = [action[..., k * rows : (k + 1) * rows, :] for k in range(fold)]
    return jnp.concatenate([prefix, jnp.concatenate(parts, axis=-1)], axis=-2)


def action_of(block, part_p, width):
    folded = block[..., part_p:, :]
    fold = folded.shape[-1] // width
    parts = [folded[..., k * width : (k + 1) * width] for k in range(fold)]
    return jnp.concatenate(parts, axis=-2)


def a2a(parts):
    return lax.all_to_all(parts, "seq", 0, 0, tiled=True)


def split_columns(weight):
    depth, width = weight.shape
    count = lax.axis_size("seq")
    return weight.reshape(depth, count, width // count).transpose(1, 0, 2)


def split_rows(weight):
    width, depth = weight.shape
    count = lax.axis_size("seq")
    return weight.reshape(count, width // count, depth)


def join_rows(parts):
    return parts.reshape(-1, parts.shape[-1])


def join_columns(parts):
    return parts.transpose(1, 0, 2).reshape(parts.shape[1], -1)


def rms_norm(values, gain_vec):
    return values * lax.rsqrt(jnp.mean(values * values, axis=-1, keepdims=True) + EPS) * gain_vec


def norm_backward(values, gain_vec, grad_normed):
    return jax.vjp(rms_norm, values, gain_vec)[1](grad_normed)


def geglu_act(gate_pre, up_pre):
    return jax.nn.gelu(gate_pre, approximate=True) * up_pre


def attend_forward(query_flat, key_rows, value_rows, keep_mask):
    row_count = query_flat.shape[0]
    head_size = key_rows.shape[1]
    query_heads = query_flat.reshape(row_count, -1, head_size)
    scores = jnp.einsum(
        "qhd,kd->hqk", query_heads, key_rows, preferred_element_type=F32
    ) * (head_size ** (-0.5))
    scores = jnp.where(keep_mask[None, None, :], scores, MASKED)
    expo = jnp.exp(scores - jnp.max(scores, axis=-1, keepdims=True))
    probs = expo / jnp.sum(expo, axis=-1, keepdims=True)
    mixed_rows = jnp.einsum(
        "hqk,kd->qhd", probs.astype(BF), value_rows, preferred_element_type=F32
    )
    return mixed_rows.reshape(row_count, -1).astype(BF), probs


def attend_backward(query_flat, key_rows, value_rows, probs, grad_mixed):
    row_count = query_flat.shape[0]
    head_size = key_rows.shape[1]
    score_scale = head_size ** (-0.5)
    query_heads = query_flat.reshape(row_count, -1, head_size)
    grad_heads = grad_mixed.reshape(row_count, -1, head_size)
    grad_probs = jnp.einsum("qhd,kd->hqk", grad_heads, value_rows, preferred_element_type=F32)
    row_inner = jnp.sum(grad_probs * probs, axis=-1, keepdims=True)
    grad_scores = (probs * (grad_probs - row_inner)).astype(BF)
    grad_query = jnp.einsum("hqk,kd->qhd", grad_scores, key_rows, preferred_element_type=F32)
    grad_query = (grad_query * score_scale).reshape(row_count, -1).astype(BF)
    grad_keys = score_scale * jnp.einsum(
        "hqk,qhd->kd", grad_scores, query_heads, preferred_element_type=F32
    )
    grad_values = jnp.einsum(
        "hqk,qhd->kd", probs.astype(BF), grad_heads, preferred_element_type=F32
    )
    return grad_query, jnp.concatenate([grad_keys, grad_values], axis=1)


def feed_forward(normed_groups, cot_groups, w_gate, w_up, w_down):
    gn_groups, mids, d_gates, d_ups = [], [], [], []
    for normed, cot in zip(normed_groups, cot_groups):
        gate_pre = dot(normed, w_gate, 1, 0)
        up_pre = dot(normed, w_up, 1, 0)
        grad_hidden = dot(cot, w_down, 1, 1)
        mid, pullback = jax.vjp(geglu_act, gate_pre, up_pre)
        d_gate, d_up = pullback(grad_hidden)
        d_gate, d_up = d_gate.astype(BF), d_up.astype(BF)
        gn_groups.append((dot(d_gate, w_gate, 1, 1) + dot(d_up, w_up, 1, 1)).astype(BF))
        mids.append(mid.astype(BF))
        d_gates.append(d_gate)
        d_ups.append(d_up)
    return gn_groups, mids, d_gates, d_ups


def weight_grad(left, right):
    return dot(left, right, 0, 0).astype(BF)


def quarters(array, axis):
    return jnp.split(array, 4, axis=axis)


def body(
    hidden_prefix,
    hidden_action,
    norm1_prefix,
    query_prefix,
    key_prefix,
    value_prefix,
    out_prefix,
    norm2_prefix,
    gate_prefix,
    up_prefix,
    down_prefix,
    norm1_action,
    query_action,
    key_action,
    value_action,
    out_action,
    norm2_action,
    gate_action,
    up_action,
    down_action,
    cot_prefix,
    cot_action,
    instr_len,
    slot_source,
):
    seq_index = lax.axis_index("seq")
    episodes = lax.axis_size("seq")
    quad = lax.axis_size("mp") * lax.axis_size("expert")
    mine = lax.axis_index("mp") * lax.axis_size("expert") + lax.axis_index("expert")
    prefix_rows, action_rows_all = hidden_prefix.shape[0], hidden_action.shape[0]
    slot_count = slot_source.shape[0]
    action_rows = action_rows_all // slot_count
    head_size = key_prefix.shape[1]
    head_cols = query_prefix.shape[1]
    part_p = -(-prefix_rows // (16 * quad)) * 16
    part_a = -(-action_rows_all // (16 * quad)) * 16
    kv_cols = 2 * head_size // quad

    positions = jnp.arange(prefix_rows, dtype=jnp.int32)
    keep_prefix = positions < IMG + instr_len[seq_index]
    live_slot = slot_source >= 0
    offsets = jnp.where(live_slot, slot_source, 0)
    source_ep = (seq_index - offsets + episodes) % episodes
    keep_slots = (positions[None, :] < IMG + instr_len[source_ep][:, None]) & live_slot[:, None]
    keep_all = jnp.concatenate(
        [keep_slots, jnp.ones((slot_count, action_rows), dtype=bool)], axis=1
    )
    from_prev = slot_source == 1
    from_here = slot_source == 0
    live_rows = jnp.repeat(live_slot.astype(F32), action_rows)[:, None]

    def own_part(rows, part):
        return lax.dynamic_slice_in_dim(pad_rows(rows, quad * part), mine * part, part, axis=0)

    x_p, x_a = own_part(hidden_prefix, part_p), own_part(hidden_action, part_a)
    x_p, x_a = x_p.astype(F32), x_a.astype(F32)
    live_a = own_part(live_rows, part_a)
    cot_p, cot_a = own_part(cot_prefix, part_p), own_part(cot_action, part_a)
    cot_live_a = (cot_a.astype(F32) * live_a).astype(BF)

    def quarter_kv(w_key, w_value):
        return lax.dynamic_slice_in_dim(
            jnp.concatenate([w_key, w_value], axis=1), mine * kv_cols, kv_cols, axis=1
        )

    early_cols = head_cols + kv_cols
    depth_p, depth_a = query_prefix.shape[0], query_action.shape[0]
    gains = jnp.concatenate([norm1_prefix, norm2_prefix, norm1_action, norm2_action])
    gain_rows = -(-gains.shape[0] // (16 * LANES)) * 16
    gain_block = jnp.pad(gains, (0, gain_rows * LANES - gains.shape[0]))
    out_both = jnp.concatenate([out_prefix, out_action], axis=1)
    out_both = jnp.pad(out_both, ((0, 0), (0, -out_both.shape[1] % LANES)))
    pieces = [
        fold(query_prefix, LANES),
        fold(quarter_kv(key_prefix, value_prefix), LANES),
        fold(query_action, LANES),
        fold(quarter_kv(key_action, value_action), LANES),
        fold(out_both, LANES),
        gain_block.reshape(gain_rows, LANES),
    ]
    early = lax.all_gather(jnp.concatenate(pieces, axis=0), "seq", axis=0, tiled=False)

    gate_p = a2a(split_columns(gate_prefix))
    gate_p, up_send = fence(gate_p, split_columns(up_prefix))
    up_p = a2a(up_send)
    gate_p = join_rows(gate_p)
    gate_far_p = swap(gate_p, "mp")

    cot_chunks = pack(cot_p, cot_live_a)
    in_action = [split_columns(gate_action), split_columns(up_action), split_rows(down_action)]
    in_action = jnp.concatenate(in_action, axis=1)
    early, up_p, gate_far_p, down_send, in_action, cot_chunks = fence(
        early, up_p, gate_far_p, split_rows(down_prefix), in_action, cot_chunks
    )
    down_p, in_action = a2a(down_send), a2a(in_action)
    up_p = join_rows(up_p)
    up_far_p = swap(up_p, "mp")
    cot_chunks = seq_gather(cot_chunks)

    starts, w_in = [0], []
    for piece in pieces:
        starts.append(starts[-1] + piece.shape[0])
    parts = [early[:, a:b] for a, b in zip(starts[:-1], starts[1:])]
    for rows, (query, kv) in ((depth_p, parts[:2]), (depth_a, parts[2:4])):
        w_in.append(join_rows(unfold(jnp.concatenate([query, kv], axis=1), rows)))
    w_in_p, w_in_a = w_in
    w_out = unfold(parts[4], head_cols)
    w_out_p = join_columns(w_out[:, :, :depth_p])
    w_out_a = join_columns(w_out[:, :, depth_p : depth_p + depth_a])
    gains = parts[5].reshape(episodes, -1)
    gain1_p = gains[:, :depth_p].reshape(-1).astype(F32)
    gain2_p = gains[:, depth_p : 2 * depth_p].reshape(-1).astype(F32)
    gain1_a = gains[:, 2 * depth_p : 2 * depth_p + depth_a].reshape(-1).astype(F32)
    gain2_a = gains[:, 2 * depth_p + depth_a : 2 * (depth_p + depth_a)].reshape(-1).astype(F32)

    normed1_p = rms_norm(hidden_prefix.astype(F32), gain1_p).astype(BF)
    normed1_a = rms_norm(hidden_action.astype(F32), gain1_a).astype(BF)
    in_p, in_a = dot(normed1_p, w_in_p, 1, 0).astype(BF), dot(normed1_a, w_in_a, 1, 0).astype(BF)
    query_p, query_a = in_p[:, :head_cols], in_a[:, :head_cols]
    kv_both = quad_gather(jnp.concatenate([in_p[:, head_cols:], in_a[:, head_cols:]], axis=0))
    kv_both = kv_both.transpose(1, 0, 2).reshape(-1, 2 * head_size)
    kv_p, kv_a = kv_both[:prefix_rows], kv_both[prefix_rows:]
    kv_prev = shift(kv_p, "seq", 1)
    keys_p, values_p = kv_p[:, :head_size], kv_p[:, head_size:]
    mixed_p, probs_p = attend_forward(query_p, keys_p, values_p, keep_prefix)
    kv_slots = jnp.where(from_prev[:, None, None], kv_prev[None], kv_p[None])
    kv_slots = jnp.concatenate([kv_slots, kv_a.reshape(slot_count, action_rows, -1)], axis=1)
    keys_slots, values_slots = kv_slots[:, :, :head_size], kv_slots[:, :, head_size:]
    query_slots = query_a.reshape(slot_count, action_rows, -1)
    mixed_slots, probs_a = jax.vmap(attend_forward)(
        query_slots, keys_slots, values_slots, keep_all
    )
    mixed_a = mixed_slots.reshape(action_rows_all, -1)
    attn_p = dot(pad_rows(mixed_p, quad * part_p), w_out_p, 1, 0).reshape(quad, part_p, -1)
    attn_a = dot(pad_rows(mixed_a, quad * part_a), w_out_a, 1, 0).reshape(quad, part_a, -1)
    attn = quad_reduce(pack(attn_p, attn_a))
    middle_p = x_p + attn[:part_p]
    middle_a = x_a + live_a * action_of(attn, part_p, x_a.shape[1])
    normed2 = pack(
        rms_norm(middle_p, gain2_p).astype(BF), rms_norm(middle_a, gain2_a).astype(BF)
    )

    normed2, down_p, in_action, up_far_p = fence(normed2, down_p, in_action, up_far_p)
    down_p = join_columns(down_p)
    down_far_p, far_action = swap(down_p, "mp"), swap(in_action, "mp")
    w_gate_p, w_up_p = quad_join(gate_p, gate_far_p, 1), quad_join(up_p, up_far_p, 1)
    w_down_p = quad_join(down_p, down_far_p, 0)
    in_action = [in_action, far_action, swap(in_action, "expert"), swap(far_action, "expert")]
    w_gate_a = cat([join_rows(part[:, :depth_a]) for part in in_action], 1)
    w_up_a = cat([join_rows(part[:, depth_a : 2 * depth_a]) for part in in_action], 1)
    w_down_a = cat([join_columns(part[:, 2 * depth_a :]) for part in in_action], 0)

    normed2_chunks = seq_gather(normed2)
    pair = 4 if on_ring() else episodes

    def prefix_groups(chunks):
        rows = [chunk[:part_p] for chunk in chunks]
        return [cat(rows[k : k + pair]) for k in range(0, episodes, pair)]

    def action_group(chunks):
        return cat([action_of(chunk, part_p, x_a.shape[1]) for chunk in chunks])

    normed2_p, normed2_a = prefix_groups(normed2_chunks), action_group(normed2_chunks)
    cot_full_p, cot_full_a = prefix_groups(cot_chunks), action_group(cot_chunks)
    gn2_p, mid_p, d_gate_p, d_up_p = feed_forward(
        normed2_p, cot_full_p, w_gate_p, w_up_p, w_down_p
    )
    gn2_a, mid_a, d_gate_a, d_up_a = feed_forward(
        [normed2_a], [cot_full_a], w_gate_a, w_up_a, w_down_a
    )
    gn2_a, mid_a, d_gate_a, d_up_a = gn2_a[0], mid_a[0], d_gate_a[0], d_up_a[0]

    def chunks_of(groups, action):
        groups = [group.reshape(pair, part_p, -1) for group in groups]
        action = action.reshape(episodes, part_a, -1)
        return [pack(groups[k // pair][k % pair], action[k]) for k in range(episodes)]

    gn2, mid_p, d_gate_p, d_up_p = fence(chunks_of(gn2_p, gn2_a), mid_p, d_gate_p, d_up_p)
    gn2 = seq_reduce(gn2)
    normed2_p, cot_full_p = cat(normed2_p), cat(cot_full_p)
    dwd_p = quad_reduce_rel(quarters(weight_grad(cat(mid_p), cot_full_p), 0))
    y_p = [dot(mid, w_down_p, 1, 0).astype(BF) for mid in mid_p]
    y_a = dot(mid_a, w_down_a, 1, 0).astype(BF)
    y_chunks = chunks_of(y_p, y_a)
    d_gate_p, d_up_p = cat(d_gate_p), cat(d_up_p)
    dwg_p = quad_reduce_rel([weight_grad(normed2_p, g) for g in quarters(d_gate_p, 1)])
    dwu_p = quad_reduce_rel([weight_grad(normed2_p, g) for g in quarters(d_up_p, 1)])
    gn2, dwd_p, y_chunks = fence(gn2, dwd_p, y_chunks)
    dwd_p = a2a(split_columns(dwd_p))
    y_sum = seq_reduce(y_chunks)
    dmid_norm_p, dgain2_p = norm_backward(middle_p, gain2_p, gn2[:part_p])
    dmid_norm_a, dgain2_a = norm_backward(
        middle_a, gain2_a, action_of(gn2, part_p, x_a.shape[1])
    )
    dmid_p = cot_p.astype(F32) + dmid_norm_p
    dmid_a = cot_a.astype(F32) + dmid_norm_a
    dao = quad_gather(pack(dmid_p.astype(BF), (dmid_a * live_a).astype(BF)))

    def whole_rows(block):
        prefix = block[:, :part_p].reshape(quad * part_p, -1)[:prefix_rows]
        action = action_of(block, part_p, x_a.shape[1]).reshape(quad * part_a, -1)
        return prefix, action[:action_rows_all]

    dao_p, dao_a = whole_rows(dao)

    dmix_p, dmix_a = dot(dao_p, w_out_p, 1, 1).astype(BF), dot(dao_a, w_out_a, 1, 1).astype(BF)
    dq_slots, dkv_slots = jax.vmap(attend_backward)(
        query_slots,
        keys_slots,
        values_slots,
        probs_a,
        dmix_a.reshape(slot_count, action_rows, -1),
    )
    dkv_pre = dkv_slots[:, :prefix_rows]
    dkv_a = dkv_slots[:, prefix_rows:].reshape(action_rows_all, -1)
    to_prev = jnp.sum(jnp.where(from_prev[:, None, None], dkv_pre, 0.0), axis=0)
    to_here = jnp.sum(jnp.where(from_here[:, None, None], dkv_pre, 0.0), axis=0)
    returned = shift(to_prev.astype(BF), "seq", -1).astype(F32)
    dq_p, dkv_p = attend_backward(query_p, keys_p, values_p, probs_p, dmix_p)
    dkv_p = dkv_p + to_here + returned
    dq_a = dq_slots.reshape(action_rows_all, -1)

    dkv_both = jnp.concatenate([dkv_p, dkv_a], axis=0)
    dkv_both, dwd_p, dwg_p, y_sum = fence(dkv_both, dwd_p, dwg_p, y_sum)
    dwg_p = a2a(split_rows(dwg_p))
    dkv_both = dkv_both.reshape(-1, quad, kv_cols).transpose(1, 0, 2)
    dkv_both = quad_reduce(dkv_both).astype(BF)
    din_p = jnp.concatenate([dq_p, dkv_both[:prefix_rows]], axis=1)
    din_a = jnp.concatenate([dq_a, dkv_both[prefix_rows:]], axis=1)
    gn1_p = dot(pad_rows(din_p, quad * part_p), w_in_p, 1, 1).reshape(quad, part_p, -1)
    gn1_a = dot(pad_rows(din_a, quad * part_a), w_in_a, 1, 1).reshape(quad, part_a, -1)
    gn1 = quad_reduce(pack(gn1_p, gn1_a))
    gn1, dwg_p, dwu_p = fence(gn1, dwg_p, dwu_p)
    dx_norm_p, dgain1_p = norm_backward(x_p, gain1_p, gn1[:part_p])
    dx_norm_a, dgain1_a = norm_backward(x_a, gain1_a, action_of(gn1, part_p, x_a.shape[1]))
    dx = quad_gather(pack((dmid_p + dx_norm_p).astype(BF), (dmid_a + dx_norm_a).astype(BF)))
    dx_p, dx_a = whole_rows(dx)
    dx_p, dx_a = dx_p.astype(F32), dx_a.astype(F32)
    y_p = middle_p + y_sum[:part_p]
    y_a = middle_a + live_a * action_of(y_sum, part_p, x_a.shape[1])
    y_out = quad_gather(pack(y_p.astype(BF), y_a.astype(BF)))
    y_p, y_a = whole_rows(y_out)

    dwd_p = join_rows(dwd_p).astype(F32)
    dwg_p = join_columns(dwg_p).astype(F32)
    dwu_p = join_columns(a2a(split_rows(dwu_p))).astype(F32)
    d_action = zip(
        quarters(weight_grad(normed2_a, d_gate_a), 1),
        quarters(weight_grad(normed2_a, d_up_a), 1),
        quarters(weight_grad(mid_a, cot_full_a), 0),
    )
    d_action = quad_reduce_rel(
        [
            jnp.concatenate([split_rows(g), split_rows(u), split_columns(d)], axis=1)
            for g, u, d in d_action
        ]
    )
    d_action = a2a(d_action).astype(F32)
    dwg_a = join_columns(d_action[:, :depth_a])
    dwu_a = join_columns(d_action[:, depth_a : 2 * depth_a])
    dwd_a = join_rows(d_action[:, 2 * depth_a :])

    dwo = jnp.concatenate(
        [
            weight_grad(mixed_p, dao_p).reshape(head_cols, episodes, -1),
            weight_grad(mixed_a, dao_a).reshape(head_cols, episodes, -1),
        ],
        axis=2,
    ).transpose(1, 0, 2)
    dwo = lax.psum_scatter(dwo, "seq", scatter_dimension=0, tiled=False).astype(F32)
    dw_in = jnp.concatenate(
        [
            weight_grad(normed1_p, din_p).reshape(episodes, -1, early_cols),
            weight_grad(normed1_a, din_a).reshape(episodes, -1, early_cols),
        ],
        axis=1,
    )
    dw_in = lax.psum_scatter(dw_in, "seq", scatter_dimension=0, tiled=False)
    dw_kv = quad_gather(dw_in[:, head_cols:]).transpose(1, 0, 2).reshape(-1, 2 * head_size)
    dw_kv = dw_kv.astype(F32)
    dw_in = dw_in.astype(F32)

    dgains = jnp.concatenate(
        [g.reshape(episodes, -1) for g in (dgain1_p, dgain2_p, dgain1_a, dgain2_a)], axis=1
    )
    dgains = seq_halve(dgains)
    return (
        y_p,
        y_a,
        dx_p,
        dx_a,
        dgains[:depth_p],
        dw_in[:depth_p, :head_cols],
        dw_kv[:depth_p, :head_size],
        dw_kv[:depth_p, head_size:],
        dwo[:, :depth_p],
        dgains[depth_p : 2 * depth_p],
        dwg_p,
        dwu_p,
        dwd_p,
        dgains[2 * depth_p : 2 * depth_p + depth_a],
        dw_in[depth_p:, :head_cols],
        dw_kv[depth_p:, :head_size],
        dw_kv[depth_p:, head_size:],
        dwo[:, depth_p:],
        dgains[2 * depth_p + depth_a :],
        dwg_a,
        dwu_a,
        dwd_a,
    )


def solution(mesh):
    rows, flat = P("seq", None), P("seq")
    wide, tall = P("seq", ("mp", "expert")), P(("mp", "expert"), "seq")
    one_expert = (flat, wide, rows, rows, tall, flat, wide, wide, tall)
    return jax.shard_map(
        body,
        mesh=mesh,
        in_specs=(rows, rows) + one_expert + one_expert + (rows, rows, P(), flat),
        out_specs=(rows, rows, rows, rows) + one_expert + one_expert,
        check_vma=False,
    )
```

```python
import math

import jax
import jax.numpy as jnp
from jax import lax
from jax.experimental import pallas as pl
from jax.experimental.pallas import tpu as pltpu
from jax.sharding import PartitionSpec as P

IMG = 512
EPS = 1e-06
MASKED = -1e30
GELU_A = (2.0 / math.pi) ** 0.5
GELU_B = 0.044715
TILE = 256
VMEM_BYTES = 60 * 2**20
BF = jnp.bfloat16
F32 = jnp.float32

SNAKE = (0, 2, 4, 6, 7, 5, 3, 1)


def dot(left, right, left_dim, right_dim):
    return lax.dot_general(
        left, right, (((left_dim,), (right_dim,)), ((), ())), preferred_element_type=F32
    )


def fence(*values):
    return lax.optimization_barrier(values)


def cat(parts, axis=0):
    return parts[0] if len(parts) == 1 else jnp.concatenate(parts, axis=axis)


def pad_rows(block, rows):
    missing = rows - block.shape[0]
    return jnp.pad(block, ((0, missing), (0, 0))) if missing else block


def shift(block, axis, distance):
    count = lax.axis_size(axis)
    return lax.ppermute(block, axis, [(i, (i + distance) % count) for i in range(count)])


def ring_step(block, step):
    pairs = [(SNAKE[i], SNAKE[(i + step) % len(SNAKE)]) for i in range(len(SNAKE))]
    return lax.ppermute(block, "seq", pairs)


def ring_owners():
    count = len(SNAKE)
    place = jnp.array([SNAKE.index(i) for i in range(count)], jnp.int32)[lax.axis_index("seq")]
    steps = [(k + 1) // 2 if k % 2 else -(k // 2) for k in range(count)]
    return jnp.array(SNAKE, jnp.int32)[(place + jnp.array(steps, jnp.int32) + count) % count]


def on_ring():
    return lax.axis_size("seq") == len(SNAKE)


class Gathered:
    def __init__(self, block):
        self.ahead, self.behind = [block], [block]

    def hop(self):
        if on_ring():
            if len(self.ahead) <= len(SNAKE) // 2:
                self.ahead.append(ring_step(self.ahead[-1], -1))
            if len(self.behind) <= (len(SNAKE) - 1) // 2:
                self.behind.append(ring_step(self.behind[-1], 1))

    def meet(self, *values):
        self.ahead[-1], self.behind[-1], *values = fence(self.ahead[-1], self.behind[-1], *values)
        return values

    def blocks_and_owners(self):
        if not on_ring():
            whole = lax.all_gather(self.ahead[0], "seq", axis=0, tiled=False)
            return [whole[k] for k in range(whole.shape[0])], None
        order = [self.ahead[0]]
        for k in range(1, len(SNAKE)):
            order.append(self.ahead[(k + 1) // 2] if k % 2 else self.behind[k // 2])
        return order, ring_owners()


class Summed:
    def __init__(self, blocks):
        self.blocks, self.left, self.done = blocks, len(blocks) - 3, False
        self.going, self.back = blocks[-1], blocks[-2]

    def hop(self):
        if not on_ring():
            return
        going = ring_step(self.going, 1).astype(F32)
        if self.left < 0:
            self.back, self.done = self.back + going, True
            return
        self.going = (going + self.blocks[self.left].astype(F32)).astype(BF)
        back = ring_step(self.back, -1).astype(F32) + self.blocks[self.left - 1].astype(F32)
        self.back = back if self.left == 1 else back.astype(BF)
        self.left -= 2

    def meet(self, *values):
        self.going, self.back, *values = fence(self.going, self.back, *values)
        return values

    def total(self):
        if on_ring():
            assert self.done
            return self.back
        return lax.psum_scatter(jnp.stack(self.blocks), "seq", scatter_dimension=0).astype(F32)


def seq_halve(rows):
    count, index = rows.shape[0], lax.axis_index("seq")
    while count > 1:
        count //= 2
        bit = (index // count) % 2
        halves = rows.reshape(2, count, -1)
        keep = lax.dynamic_index_in_dim(halves, bit, 0, keepdims=False)
        give = lax.dynamic_index_in_dim(halves, 1 - bit, 0, keepdims=False)
        pairs = [(i, i ^ count) for i in range(lax.axis_size("seq"))]
        rows = keep + lax.ppermute(give, "seq", pairs)
    rows = rows + shift(rows, "expert", 1)
    return (rows + shift(rows, "mp", 1)).reshape(-1)


def swap(block, axis):
    return shift(block, axis, 1)


def quad_join(block, across, axis):
    return cat([block, across, swap(block, "expert"), swap(across, "expert")], axis)


def quad_gather(block):
    m, e = lax.axis_index("mp"), lax.axis_index("expert")
    across = swap(block, "mp")
    mine = jnp.where(m == 0, jnp.stack([block, across]), jnp.stack([across, block]))
    other = swap(mine, "expert")
    both = jnp.where(e == 0, jnp.stack([mine, other], 1), jnp.stack([other, mine], 1))
    return both.reshape((4,) + block.shape)


def quad_reduce(whole):
    m, e = lax.axis_index("mp"), lax.axis_index("expert")
    parts = whole.reshape((2, 2) + whole.shape[1:])
    give = lax.dynamic_index_in_dim(parts, 1 - e, 1, keepdims=False).astype(BF)
    keep = lax.dynamic_index_in_dim(parts, e, 1, keepdims=False).astype(F32)
    pair = keep + swap(give, "expert").astype(F32)
    give = lax.dynamic_index_in_dim(pair, 1 - m, 0, keepdims=False).astype(BF)
    keep = lax.dynamic_index_in_dim(pair, m, 0, keepdims=False)
    return keep + swap(give, "mp").astype(F32)


def pair_reduce_rel(parts):
    keep = parts[0].astype(F32) + swap(parts[2].astype(BF), "expert").astype(F32)
    give = parts[1].astype(F32) + swap(parts[3].astype(BF), "expert").astype(F32)
    return keep.astype(BF), give.astype(BF)


def across_reduce(keep, give):
    return (keep.astype(F32) + swap(give, "mp").astype(F32)).astype(BF)


def pack(prefix, action):
    fold = prefix.shape[-1] // action.shape[-1]
    rows = action.shape[-2] // fold
    parts = [action[..., k * rows : (k + 1) * rows, :] for k in range(fold)]
    return jnp.concatenate([prefix, jnp.concatenate(parts, axis=-1)], axis=-2)


def action_of(block, part_p, width):
    folded = block[..., part_p:, :]
    fold = folded.shape[-1] // width
    parts = [folded[..., k * width : (k + 1) * width] for k in range(fold)]
    return jnp.concatenate(parts, axis=-2)


def a2a(parts):
    return lax.all_to_all(parts, "seq", 0, 0, tiled=True)


def split_columns(weight):
    depth, width = weight.shape
    count = lax.axis_size("seq")
    return weight.reshape(depth, count, width // count).transpose(1, 0, 2)


def split_rows(weight):
    width, depth = weight.shape
    count = lax.axis_size("seq")
    return weight.reshape(count, width // count, depth)


def join_rows(parts):
    return parts.reshape(-1, parts.shape[-1])


def join_columns(parts):
    return parts.transpose(1, 0, 2).reshape(parts.shape[1], -1)


def rms_norm(values, gain_vec):
    return values * lax.rsqrt(jnp.mean(values * values, axis=-1, keepdims=True) + EPS) * gain_vec


def norm_backward(values, gain_vec, grad_normed):
    return jax.vjp(rms_norm, values, gain_vec)[1](grad_normed)


def geglu_act(gate_pre, up_pre):
    return jax.nn.gelu(gate_pre, approximate=True) * up_pre


def attend_forward(query_flat, key_rows, value_rows, keep_mask):
    row_count = query_flat.shape[0]
    head_size = key_rows.shape[1]
    query_heads = query_flat.reshape(row_count, -1, head_size)
    scores = jnp.einsum(
        "qhd,kd->hqk", query_heads, key_rows, preferred_element_type=F32
    ) * (head_size ** (-0.5))
    scores = jnp.where(keep_mask[None, None, :], scores, MASKED)
    expo = jnp.exp(scores - jnp.max(scores, axis=-1, keepdims=True))
    probs = expo / jnp.sum(expo, axis=-1, keepdims=True)
    mixed_rows = jnp.einsum(
        "hqk,kd->qhd", probs.astype(BF), value_rows, preferred_element_type=F32
    )
    return mixed_rows.reshape(row_count, -1).astype(BF), probs


def attend_backward(query_flat, key_rows, value_rows, probs, grad_mixed):
    row_count = query_flat.shape[0]
    head_size = key_rows.shape[1]
    score_scale = head_size ** (-0.5)
    query_heads = query_flat.reshape(row_count, -1, head_size)
    grad_heads = grad_mixed.reshape(row_count, -1, head_size)
    grad_probs = jnp.einsum("qhd,kd->hqk", grad_heads, value_rows, preferred_element_type=F32)
    row_inner = jnp.sum(grad_probs * probs, axis=-1, keepdims=True)
    grad_scores = (probs * (grad_probs - row_inner)).astype(BF)
    grad_query = jnp.einsum("hqk,kd->qhd", grad_scores, key_rows, preferred_element_type=F32)
    grad_query = (grad_query * score_scale).reshape(row_count, -1).astype(BF)
    grad_keys = score_scale * jnp.einsum(
        "hqk,qhd->kd", grad_scores, query_heads, preferred_element_type=F32
    )
    grad_values = jnp.einsum(
        "hqk,qhd->kd", probs.astype(BF), grad_heads, preferred_element_type=F32
    )
    return grad_query, jnp.concatenate([grad_keys, grad_values], axis=1)


def gelu_parts(gate):
    square = gate * gate
    bend = jnp.tanh(gate * (GELU_A + (GELU_A * GELU_B) * square))
    half = 0.5 + 0.5 * bend
    act = gate * half
    return act, half + act * (1.0 - bend) * (GELU_A + (3.0 * GELU_A * GELU_B) * square)


def feed_back(normed, cot, w_gate, w_up, w_down):
    gate, up, grad = dot(normed, w_gate, 1, 0), dot(normed, w_up, 1, 0), dot(cot, w_down, 1, 1)
    act, slope = gelu_parts(gate)
    return (act * up).astype(BF), (grad * up * slope).astype(BF), (grad * act).astype(BF)


def whole_block(shape):
    return pl.BlockSpec(shape, lambda j, *_: (0,) * len(shape), pipeline_mode=pl.Buffered(1))


def column_block(rows, tile):
    return pl.BlockSpec((rows, tile), lambda j, *_: (0, j))


def row_block(tile, columns):
    return pl.BlockSpec((tile, columns), lambda j, *_: (j, 0))


def row_kernel(body, count, ins, outs, flops, name, order=(), scratch=()):
    moved = sum(math.prod(a.shape) * a.dtype.itemsize for a, _ in ins + outs)
    return pl.pallas_call(
        body,
        grid_spec=pltpu.PrefetchScalarGridSpec(
            num_scalar_prefetch=len(order),
            grid=(count,),
            in_specs=[spec for _, spec in ins],
            out_specs=[spec for _, spec in outs],
            scratch_shapes=scratch,
        ),
        out_shape=[shape for shape, _ in outs],
        compiler_params=pltpu.CompilerParams(vmem_limit_bytes=VMEM_BYTES),
        cost_estimate=pl.CostEstimate(flops=flops, transcendentals=0, bytes_accessed=moved),
        name=name,
    )(*order, *[a for a, _ in ins])


def like(rows, columns):
    return jax.ShapeDtypeStruct((rows, columns), BF)


def feed_inner(normed, cots, part, w_gate, w_up, w_down, width_a):
    depth, width = w_gate[0].shape[0], 4 * w_gate[0].shape[1]
    normed, order = normed.blocks_and_owners()
    count, packed = cots.shape[0], cots.shape[1]
    rows, part_a = count * part, (packed - part) * depth // width_a
    if not on_ring():
        whole = jnp.stack(normed)
        joined = [block[:, :part].reshape(rows, depth) for block in (whole, cots)]
        action = [action_of(block, part, width_a).reshape(-1, width_a) for block in (whole, cots)]
        weights = cat(w_gate, 1), cat(w_up, 1), cat(w_down, 0)
        return feed_back(*joined, *weights), joined, action

    def place(block, owner, out_ref, action_ref):
        out_ref[pl.ds(pl.multiple_of(owner * part, 16), part), :] = block[:part, :]
        for k in range(depth // width_a):
            at = pl.multiple_of(owner * part_a + k * (packed - part), 16)
            columns = pl.ds(k * width_a, width_a)
            action_ref[pl.ds(at, packed - part), :] = block[part:packed, columns]

    steps = width // 4 // TILE

    def body(order_ref, *refs):
        cot_ref, weights = refs[count], refs[count + 1 : count + 13]
        mid_ref, dg_ref, du_ref, n_ref, c_ref, na_ref, ca_ref = refs[count + 13 : count + 20]
        chosen = refs[count + 20 :]

        @pl.when(pl.program_id(0) == 0)
        def _():
            for k in range(count):
                place(refs[k], order_ref[k], n_ref, na_ref)
                place(cot_ref.at[k], k, c_ref, ca_ref)

        for q in range(4):

            @pl.when(pl.program_id(0) // steps == q)
            def _():
                for k in range(3):
                    chosen[k][...] = weights[4 * k + q][...]

        mid_ref[...], dg_ref[...], du_ref[...] = feed_back(
            n_ref[...], c_ref[...], *[ref[...] for ref in chosen]
        )

    def part_of(q, axis):
        def index(j, *_):
            at = jnp.clip(j - q * steps, 0, steps - 1)
            return (0, at) if axis else (at, 0)

        return pl.BlockSpec((depth, TILE) if axis else (TILE, depth), index)

    ins = [(block, whole_block((packed, depth))) for block in normed]
    ins += [(cots, whole_block((count, packed, depth)))]
    ins += [(w_gate[q], part_of(q, 1)) for q in range(4)]
    ins += [(w_up[q], part_of(q, 1)) for q in range(4)]
    ins += [(w_down[q], part_of(q, 0)) for q in range(4)]
    outs = [(like(rows, width), column_block(rows, TILE))] * 3
    outs += [(like(rows, depth), whole_block((rows, depth)))] * 2
    outs += [(like(count * part_a, width_a), whole_block((count * part_a, width_a)))] * 2
    scratch = [pltpu.VMEM((depth, TILE), BF)] * 2 + [pltpu.VMEM((TILE, depth), BF)]
    flops = 6 * rows * depth * width
    out = row_kernel(body, width // TILE, ins, outs, flops, "feed_inner", (order,), scratch)
    return out[:3], out[3:5], out[5:]


def feed_outer(d_gate, d_up, w_gate, w_up):
    if not on_ring():
        return (dot(d_gate, cat(w_gate, 1), 1, 1) + dot(d_up, cat(w_up, 1), 1, 1)).astype(BF)
    (rows, width), depth = d_gate.shape, w_gate[0].shape[0]

    def body(dg_ref, du_ref, *refs):
        gate, up = (cat([ref[...] for ref in refs[k : k + 4]], 1) for k in (0, 4))
        total = dot(dg_ref[...], gate, 1, 1) + dot(du_ref[...], up, 1, 1)
        refs[8][...] = total.astype(BF)

    ins = [(d_gate, whole_block((rows, width))), (d_up, whole_block((rows, width)))]
    ins += [(part, row_block(TILE, width // 4)) for part in list(w_gate) + list(w_up)]
    outs = [(like(rows, depth), column_block(rows, TILE))]
    return row_kernel(body, depth // TILE, ins, outs, 4 * rows * depth * width, "feed_outer")[0]


def feed_down(mid, w_down):
    if not on_ring():
        return dot(mid, cat(w_down, 0), 1, 0).astype(BF)
    (rows, width), depth = mid.shape, w_down[0].shape[1]

    def body(mid_ref, *refs):
        weight = cat([ref[...] for ref in refs[:4]], 0)
        refs[4][...] = dot(mid_ref[...], weight, 1, 0).astype(BF)

    ins = [(mid, whole_block((rows, width)))]
    ins += [(part, column_block(width // 4, TILE)) for part in w_down]
    outs = [(like(rows, depth), column_block(rows, TILE))]
    return row_kernel(body, depth // TILE, ins, outs, 2 * rows * depth * width, "feed_down")[0]


def weight_grad(left, right):
    return dot(left, right, 0, 0).astype(BF)


def quarters(array, axis):
    return jnp.split(array, 4, axis=axis)


def quarter_grads(left, right):
    if not on_ring():
        return quarters(weight_grad(left, right), 1)
    (rows, depth), width = left.shape, right.shape[1]

    def body(left_ref, right_ref, *out_refs):
        out = dot(left_ref[...], right_ref[...], 0, 0).astype(BF)
        for k, out_ref in enumerate(out_refs):
            out_ref[...] = out[:, k * (width // 4) : (k + 1) * (width // 4)]

    ins = [(left, column_block(rows, TILE)), (right, whole_block((rows, width)))]
    outs = [(like(depth, width // 4), row_block(TILE, width // 4))] * 4
    return row_kernel(body, depth // TILE, ins, outs, 2 * rows * depth * width, "feed_grads")


def body(
    hidden_prefix,
    hidden_action,
    norm1_prefix,
    query_prefix,
    key_prefix,
    value_prefix,
    out_prefix,
    norm2_prefix,
    gate_prefix,
    up_prefix,
    down_prefix,
    norm1_action,
    query_action,
    key_action,
    value_action,
    out_action,
    norm2_action,
    gate_action,
    up_action,
    down_action,
    cot_prefix,
    cot_action,
    instr_len,
    slot_source,
):
    seq_index = lax.axis_index("seq")
    episodes = lax.axis_size("seq")
    quad = lax.axis_size("mp") * lax.axis_size("expert")
    mine = lax.axis_index("mp") * lax.axis_size("expert") + lax.axis_index("expert")
    prefix_rows, action_rows_all = hidden_prefix.shape[0], hidden_action.shape[0]
    slot_count = slot_source.shape[0]
    action_rows = action_rows_all // slot_count
    head_size = key_prefix.shape[1]
    head_cols = query_prefix.shape[1]
    part_p = -(-prefix_rows // (16 * quad)) * 16
    part_a = -(-action_rows_all // (16 * quad)) * 16
    kv_cols = 2 * head_size // quad

    positions = jnp.arange(prefix_rows, dtype=jnp.int32)
    keep_prefix = positions < IMG + instr_len[seq_index]
    live_slot = slot_source >= 0
    offsets = jnp.where(live_slot, slot_source, 0)
    source_ep = (seq_index - offsets + episodes) % episodes
    keep_slots = (positions[None, :] < IMG + instr_len[source_ep][:, None]) & live_slot[:, None]
    keep_all = jnp.concatenate(
        [keep_slots, jnp.ones((slot_count, action_rows), dtype=bool)], axis=1
    )
    from_prev = slot_source == 1
    from_here = slot_source == 0
    live_rows = jnp.repeat(live_slot.astype(F32), action_rows)[:, None]

    def own_part(rows, part):
        return lax.dynamic_slice_in_dim(pad_rows(rows, quad * part), mine * part, part, axis=0)

    x_p, x_a = own_part(hidden_prefix, part_p), own_part(hidden_action, part_a)
    x_p, x_a = x_p.astype(F32), x_a.astype(F32)
    live_a = own_part(live_rows, part_a)
    cot_p, cot_a = own_part(cot_prefix, part_p), own_part(cot_action, part_a)
    cot_block = pack(cot_p, (cot_a.astype(F32) * live_a).astype(BF))

    def quarter_kv(w_key, w_value):
        return lax.dynamic_slice_in_dim(
            jnp.concatenate([w_key, w_value], axis=1), mine * kv_cols, kv_cols, axis=1
        )

    early_cols = head_cols + kv_cols
    depth_p, depth_a = query_prefix.shape[0], query_action.shape[0]
    gains = jnp.concatenate([norm1_prefix, norm2_prefix, norm1_action, norm2_action])
    gain_rows = -(-gains.shape[0] // (16 * early_cols)) * 16
    gain_block = jnp.pad(gains, (0, gain_rows * early_cols - gains.shape[0]))
    early = jnp.concatenate(
        [
            jnp.concatenate([query_prefix, quarter_kv(key_prefix, value_prefix)], axis=1),
            jnp.concatenate([query_action, quarter_kv(key_action, value_action)], axis=1),
            gain_block.reshape(gain_rows, early_cols),
        ],
        axis=0,
    )
    early = lax.all_gather(early, "seq", axis=0, tiled=False)
    in_action = [split_columns(gate_action), split_columns(up_action), split_rows(down_action)]
    in_action = jnp.concatenate(in_action, axis=1)
    late = jnp.concatenate([out_prefix, out_action], axis=1)
    late = lax.all_gather(late, "seq", axis=0, tiled=False)

    gate_p = join_rows(a2a(split_columns(gate_prefix)))
    gate_other = swap(gate_p, "expert")
    early, gate_other = fence(early, gate_other)
    w_in_p = early[:, :depth_p].reshape(-1, early_cols)
    w_in_a = early[:, depth_p : depth_p + depth_a].reshape(-1, early_cols)
    gains = early[:, depth_p + depth_a :].reshape(episodes, -1)
    gain1_p = gains[:, :depth_p].reshape(-1).astype(F32)
    gain2_p = gains[:, depth_p : 2 * depth_p].reshape(-1).astype(F32)
    gain1_a = gains[:, 2 * depth_p : 2 * depth_p + depth_a].reshape(-1).astype(F32)
    gain2_a = gains[:, 2 * depth_p + depth_a : 2 * (depth_p + depth_a)].reshape(-1).astype(F32)

    normed1_p = rms_norm(hidden_prefix.astype(F32), gain1_p).astype(BF)
    normed1_a = rms_norm(hidden_action.astype(F32), gain1_a).astype(BF)
    in_p, in_a = dot(normed1_p, w_in_p, 1, 0).astype(BF), dot(normed1_a, w_in_a, 1, 0).astype(BF)
    kv_prev = shift(in_p[:, head_cols:], "seq", 1)
    kv_own = jnp.concatenate([in_p[:, head_cols:], in_a[:, head_cols:]], axis=0)

    def whole_kv(quarter):
        return quad_gather(quarter).transpose(1, 0, 2).reshape(-1, 2 * head_size)

    kv_own = whole_kv(kv_own)
    in_p, in_a, kv_own, kv_prev, gate_p, up_p, cot_block = fence(
        in_p, in_a, kv_own, kv_prev, gate_p, split_columns(up_prefix), cot_block
    )
    gate_far = swap(gate_p, "mp")
    query_p, query_a = in_p[:, :head_cols], in_a[:, :head_cols]
    up_p = a2a(up_p)
    cots = lax.all_gather(cot_block, "seq", axis=0, tiled=False)
    kv_prev = whole_kv(kv_prev)
    kv_p, kv_a = kv_own[:prefix_rows], kv_own[prefix_rows:]
    keys_p, values_p = kv_p[:, :head_size], kv_p[:, head_size:]
    mixed_p, probs_p = attend_forward(query_p, keys_p, values_p, keep_prefix)
    kv_slots = jnp.where(from_prev[:, None, None], kv_prev[None], kv_p[None])
    kv_slots = jnp.concatenate([kv_slots, kv_a.reshape(slot_count, action_rows, -1)], axis=1)
    keys_slots, values_slots = kv_slots[:, :, :head_size], kv_slots[:, :, head_size:]
    query_slots = query_a.reshape(slot_count, action_rows, -1)
    mixed_slots, probs_a = jax.vmap(attend_forward)(
        query_slots, keys_slots, values_slots, keep_all
    )
    mixed_a = mixed_slots.reshape(action_rows_all, -1)
    mixed_p, mixed_a, up_p, gate_far, down_p = fence(
        mixed_p, mixed_a, up_p, gate_far, split_rows(down_prefix)
    )
    down_p, up_p = a2a(down_p), join_rows(up_p)
    gate_far_other = swap(gate_far, "expert")
    up_far, up_other = swap(up_p, "mp"), swap(up_p, "expert")
    w_gate_p = [gate_p, gate_far, gate_other, gate_far_other]
    w_out_p = join_columns(late[:, :, :depth_p])
    w_out_a = join_columns(late[:, :, depth_p:])
    attn_p = dot(pad_rows(mixed_p, quad * part_p), w_out_p, 1, 0).reshape(quad, part_p, -1)
    attn_a = dot(pad_rows(mixed_a, quad * part_a), w_out_a, 1, 0).reshape(quad, part_a, -1)
    attn, up_far, up_other = fence(pack(attn_p, attn_a), up_far, up_other)
    attn, down_p = fence(quad_reduce(attn), down_p)
    down_p = join_columns(down_p)
    down_far, down_other = swap(down_p, "mp"), swap(down_p, "expert")
    middle_p = x_p + attn[:part_p]
    middle_a = x_a + live_a * action_of(attn, part_p, x_a.shape[1])
    normed2 = Gathered(
        pack(rms_norm(middle_p, gain2_p).astype(BF), rms_norm(middle_a, gain2_a).astype(BF))
    )
    normed2.hop()
    w_up_p = [up_p, up_far, up_other, swap(up_far, "expert")]
    w_up_p = normed2.meet(w_up_p)[0]
    normed2.hop()
    normed2.meet()
    normed2.hop()
    down_far, down_other = normed2.meet(down_far, down_other)
    normed2.hop()
    w_down_p = [down_p, down_far, down_other, swap(down_far, "expert")]
    w_down_p, cots, in_action = normed2.meet(w_down_p, cots, in_action)
    in_action = a2a(in_action)

    inner, (normed2_p, cots_p), (normed2_a, cots_a) = feed_inner(
        normed2, cots, part_p, w_gate_p, w_up_p, w_down_p, x_a.shape[1]
    )
    mid_p, d_gate_p, d_up_p = inner
    mid_p, d_gate_p, d_up_p, in_action = fence(mid_p, d_gate_p, d_up_p, in_action)
    far_action = swap(in_action, "mp")
    dwd_p = quarters(weight_grad(mid_p, cots_p), 0)
    dwd_p, mid_p, far_action = fence(dwd_p, mid_p, far_action)
    dwd_p, y_sum = pair_reduce_rel(dwd_p), feed_down(mid_p, w_down_p)
    in_action = [in_action, far_action, swap(in_action, "expert"), swap(far_action, "expert")]
    dwd_p, y_sum, d_gate_p, in_action = fence(dwd_p, y_sum, d_gate_p, in_action)
    y_sum = y_sum.reshape(episodes, part_p, -1)
    y_sum = lax.psum_scatter(y_sum, "seq", scatter_dimension=0).astype(F32)
    dwd_p, dwg_p = across_reduce(*dwd_p), quarter_grads(normed2_p, d_gate_p)
    w_gate_a = cat([join_rows(part[:, :depth_a]) for part in in_action], 1)
    w_up_a = cat([join_rows(part[:, depth_a : 2 * depth_a]) for part in in_action], 1)
    w_down_a = cat([join_columns(part[:, 2 * depth_a :]) for part in in_action], 0)
    mid_a, d_gate_a, d_up_a = feed_back(normed2_a, cots_a, w_gate_a, w_up_a, w_down_a)
    gn2_a = (dot(d_gate_a, w_gate_a, 1, 1) + dot(d_up_a, w_up_a, 1, 1)).astype(BF)
    y_a = dot(mid_a, w_down_a, 1, 0).astype(BF)
    d_action = zip(
        quarters(weight_grad(normed2_a, d_gate_a), 1),
        quarters(weight_grad(normed2_a, d_up_a), 1),
        quarters(weight_grad(mid_a, cots_a), 0),
    )
    d_action = [
        jnp.concatenate([split_rows(g), split_rows(u), split_columns(d)], axis=1)
        for g, u, d in d_action
    ]
    dwd_p, dwg_p, d_gate_p, d_up_p, d_action = fence(dwd_p, dwg_p, d_gate_p, d_up_p, d_action)
    dwd_p, dwg_p = a2a(split_columns(dwd_p)), pair_reduce_rel(dwg_p)
    dwu_p, d_action = quarter_grads(normed2_p, d_up_p), pair_reduce_rel(d_action)
    dwg_p, dwu_p, d_gate_p, d_up_p, d_action = fence(dwg_p, dwu_p, d_gate_p, d_up_p, d_action)
    dwg_p, dwu_p = across_reduce(*dwg_p), pair_reduce_rel(dwu_p)
    d_action = across_reduce(*d_action)
    gn2_p = feed_outer(d_gate_p, d_up_p, w_gate_p, w_up_p).reshape(episodes, part_p, -1)
    gn2_a, y_a = gn2_a.reshape(episodes, part_a, -1), y_a.reshape(episodes, part_a, -1)
    owners = ring_owners() if on_ring() else range(episodes)
    chunks = [pack(pack(gn2_p[k], gn2_a[k]), y_a[k]) for k in [owners[k] for k in range(episodes)]]
    chunks, dwd_p, dwg_p, dwu_p, y_sum, d_action = fence(
        chunks, dwd_p, dwg_p, dwu_p, y_sum, d_action
    )
    gn2 = Summed(chunks)
    gn2.hop()
    dwu_p = across_reduce(*dwu_p)
    gn2.meet()
    gn2.hop()
    gn2.meet()
    gn2.hop()
    dwu_p = gn2.meet(dwu_p)[0]
    gn2.hop()
    gn2, dwg_p, d_action = fence(gn2.total(), dwg_p, d_action)
    d_action = a2a(d_action).astype(F32)
    packed = x_p.shape[0] + x_a.shape[0] * x_a.shape[1] // x_p.shape[1]
    y_a = action_of(gn2, packed, x_a.shape[1])
    gn2 = gn2[:packed]

    dmid_norm_p, dgain2_p = norm_backward(middle_p, gain2_p, gn2[:part_p])
    dmid_norm_a, dgain2_a = norm_backward(
        middle_a, gain2_a, action_of(gn2, part_p, x_a.shape[1])
    )
    dmid_p = cot_p.astype(F32) + dmid_norm_p
    dmid_a = cot_a.astype(F32) + dmid_norm_a
    dao = quad_gather(pack(dmid_p.astype(BF), (dmid_a * live_a).astype(BF)))

    def whole_rows(block):
        prefix = block[:, :part_p].reshape(quad * part_p, -1)[:prefix_rows]
        action = action_of(block, part_p, x_a.shape[1]).reshape(quad * part_a, -1)
        return prefix, action[:action_rows_all]

    dao_p, dao_a = whole_rows(dao)
    dao_p, dao_a, dwg_p, d_action = fence(dao_p, dao_a, dwg_p, d_action)
    dwg_p = a2a(split_rows(dwg_p))

    dwo = jnp.concatenate(
        [
            weight_grad(mixed_p, dao_p).reshape(head_cols, episodes, -1),
            weight_grad(mixed_a, dao_a).reshape(head_cols, episodes, -1),
        ],
        axis=2,
    ).transpose(1, 0, 2)
    dwo = lax.psum_scatter(dwo, "seq", scatter_dimension=0, tiled=False).astype(F32)
    dmix_p, dmix_a = dot(dao_p, w_out_p, 1, 1).astype(BF), dot(dao_a, w_out_a, 1, 1).astype(BF)
    dq_slots, dkv_slots = jax.vmap(attend_backward)(
        query_slots,
        keys_slots,
        values_slots,
        probs_a,
        dmix_a.reshape(slot_count, action_rows, -1),
    )
    dkv_pre = dkv_slots[:, :prefix_rows]
    dkv_a = dkv_slots[:, prefix_rows:].reshape(action_rows_all, -1)
    to_prev = jnp.sum(jnp.where(from_prev[:, None, None], dkv_pre, 0.0), axis=0)
    to_here = jnp.sum(jnp.where(from_here[:, None, None], dkv_pre, 0.0), axis=0)

    def own_quarter(rows):
        return quad_reduce(rows.reshape(-1, quad, kv_cols).transpose(1, 0, 2))

    returned = own_quarter(jnp.concatenate([to_prev, dkv_a], axis=0))
    dkv_a = returned[prefix_rows:].astype(BF)
    returned = shift(returned[:prefix_rows].astype(BF), "seq", -1)
    returned, dkv_a, dmix_p, dwg_p, dwu_p = fence(returned, dkv_a, dmix_p, dwg_p, dwu_p)
    dwu_p = a2a(split_rows(dwu_p))
    dq_p, dkv_p = attend_backward(query_p, keys_p, values_p, probs_p, dmix_p)
    dkv_p = dkv_p + to_here
    dq_a = dq_slots.reshape(action_rows_all, -1)

    dkv_p = (own_quarter(dkv_p) + returned.astype(F32)).astype(BF)
    din_p = jnp.concatenate([dq_p, dkv_p], axis=1)
    din_a = jnp.concatenate([dq_a, dkv_a], axis=1)
    gn1_p = dot(pad_rows(din_p, quad * part_p), w_in_p, 1, 1).reshape(quad, part_p, -1)
    gn1_a = dot(pad_rows(din_a, quad * part_a), w_in_a, 1, 1).reshape(quad, part_a, -1)
    gn1 = quad_reduce(pack(gn1_p, gn1_a))
    gn1, dwu_p, dwo = fence(gn1, dwu_p, dwo)
    dx_norm_p, dgain1_p = norm_backward(x_p, gain1_p, gn1[:part_p])
    dx_norm_a, dgain1_a = norm_backward(x_a, gain1_a, action_of(gn1, part_p, x_a.shape[1]))
    dx = quad_gather(pack((dmid_p + dx_norm_p).astype(BF), (dmid_a + dx_norm_a).astype(BF)))
    dx_p, dx_a = whole_rows(dx)
    dx_p, dx_a = dx_p.astype(F32), dx_a.astype(F32)
    y_p, y_a = middle_p + y_sum, middle_a + live_a * y_a
    y_out = quad_gather(pack(y_p.astype(BF), y_a.astype(BF)))
    y_p, y_a = whole_rows(y_out)

    dwd_p = join_rows(dwd_p).astype(F32)
    dwg_p = join_columns(dwg_p).astype(F32)
    dwu_p = join_columns(dwu_p).astype(F32)
    dwg_a = join_columns(d_action[:, :depth_a])
    dwu_a = join_columns(d_action[:, depth_a : 2 * depth_a])
    dwd_a = join_rows(d_action[:, 2 * depth_a :])

    dw_in = jnp.concatenate(
        [
            weight_grad(normed1_p, din_p).reshape(episodes, -1, early_cols),
            weight_grad(normed1_a, din_a).reshape(episodes, -1, early_cols),
        ],
        axis=1,
    )
    dw_in = lax.psum_scatter(dw_in, "seq", scatter_dimension=0, tiled=False)
    dw_kv = quad_gather(dw_in[:, head_cols:]).transpose(1, 0, 2).reshape(-1, 2 * head_size)
    dw_kv = dw_kv.astype(F32)
    dw_in = dw_in.astype(F32)

    dgains = jnp.concatenate(
        [g.reshape(episodes, -1) for g in (dgain1_p, dgain2_p, dgain1_a, dgain2_a)], axis=1
    )
    dgains = seq_halve(dgains)
    return (
        y_p,
        y_a,
        dx_p,
        dx_a,
        dgains[:depth_p],
        dw_in[:depth_p, :head_cols],
        dw_kv[:depth_p, :head_size],
        dw_kv[:depth_p, head_size:],
        dwo[:, :depth_p],
        dgains[depth_p : 2 * depth_p],
        dwg_p,
        dwu_p,
        dwd_p,
        dgains[2 * depth_p : 2 * depth_p + depth_a],
        dw_in[depth_p:, :head_cols],
        dw_kv[depth_p:, :head_size],
        dw_kv[depth_p:, head_size:],
        dwo[:, depth_p:],
        dgains[2 * depth_p + depth_a :],
        dwg_a,
        dwu_a,
        dwd_a,
    )


def solution(mesh):
    rows, flat = P("seq", None), P("seq")
    wide, tall = P("seq", ("mp", "expert")), P(("mp", "expert"), "seq")
    one_expert = (flat, wide, rows, rows, tall, flat, wide, wide, tall)
    return jax.shard_map(
        body,
        mesh=mesh,
        in_specs=(rows, rows) + one_expert + one_expert + (rows, rows, P(), flat),
        out_specs=(rows, rows, rows, rows) + one_expert + one_expert,
        check_vma=False,
    )
```

```python
import math

import jax
import jax.numpy as jnp
from jax import lax
from jax.experimental import pallas as pl
from jax.experimental.pallas import tpu as pltpu
from jax.sharding import PartitionSpec as P

IMG = 512
EPS = 1e-06
MASKED = -1e30
GELU_A = (2.0 / math.pi) ** 0.5
GELU_B = 0.044715
TILE = 256
VMEM_BYTES = 60 * 2**20
SHARE = 1000
BF = jnp.bfloat16
F32 = jnp.float32

SNAKE = (0, 2, 4, 6, 7, 5, 3, 1)


def dot(left, right, left_dim, right_dim):
    return lax.dot_general(
        left, right, (((left_dim,), (right_dim,)), ((), ())), preferred_element_type=F32
    )


def fence(*values):
    return lax.optimization_barrier(values)


def cat(parts, axis=0):
    return parts[0] if len(parts) == 1 else jnp.concatenate(parts, axis=axis)


def pad_rows(block, rows):
    missing = rows - block.shape[0]
    return jnp.pad(block, ((0, missing), (0, 0))) if missing else block


def shift(block, axis, distance):
    count = lax.axis_size(axis)
    return lax.ppermute(block, axis, [(i, (i + distance) % count) for i in range(count)])


def ring_step(block, step):
    pairs = [(SNAKE[i], SNAKE[(i + step) % len(SNAKE)]) for i in range(len(SNAKE))]
    return lax.ppermute(block, "seq", pairs)


def ring_owners():
    count = len(SNAKE)
    place = jnp.array([SNAKE.index(i) for i in range(count)], jnp.int32)[lax.axis_index("seq")]
    steps = [(k + 1) // 2 if k % 2 else -(k // 2) for k in range(count)]
    return jnp.array(SNAKE, jnp.int32)[(place + jnp.array(steps, jnp.int32) + count) % count]


def on_ring():
    return lax.axis_size("seq") == len(SNAKE)


class Gathered:
    def __init__(self, block):
        self.ahead, self.behind = [block], [block]

    def hop(self):
        if on_ring():
            if len(self.ahead) <= len(SNAKE) // 2:
                self.ahead.append(ring_step(self.ahead[-1], -1))
            if len(self.behind) <= (len(SNAKE) - 1) // 2:
                self.behind.append(ring_step(self.behind[-1], 1))

    def meet(self, *values):
        self.ahead[-1], self.behind[-1], *values = fence(self.ahead[-1], self.behind[-1], *values)
        return values

    def blocks_and_owners(self):
        if not on_ring():
            whole = lax.all_gather(self.ahead[0], "seq", axis=0, tiled=False)
            return [whole[k] for k in range(whole.shape[0])], None
        order = [self.ahead[0]]
        for k in range(1, len(SNAKE)):
            order.append(self.ahead[(k + 1) // 2] if k % 2 else self.behind[k // 2])
        return order, ring_owners()


class Summed:
    def __init__(self, blocks):
        self.blocks, self.left, self.done = blocks, len(blocks) - 3, False
        self.going, self.back = blocks[-1], blocks[-2]

    def hop(self):
        if not on_ring():
            return
        going = ring_step(self.going, 1).astype(F32)
        if self.left < 0:
            self.back, self.done = self.back + going, True
            return
        self.going = (going + self.blocks[self.left].astype(F32)).astype(BF)
        back = ring_step(self.back, -1).astype(F32) + self.blocks[self.left - 1].astype(F32)
        self.back = back if self.left == 1 else back.astype(BF)
        self.left -= 2

    def meet(self, *values):
        self.going, self.back, *values = fence(self.going, self.back, *values)
        return values

    def total(self):
        if on_ring():
            assert self.done
            return self.back
        return lax.psum_scatter(jnp.stack(self.blocks), "seq", scatter_dimension=0).astype(F32)


def seq_halve(rows):
    count, index = rows.shape[0], lax.axis_index("seq")
    while count > 1:
        count //= 2
        bit = (index // count) % 2
        halves = rows.reshape(2, count, -1)
        keep = lax.dynamic_index_in_dim(halves, bit, 0, keepdims=False)
        give = lax.dynamic_index_in_dim(halves, 1 - bit, 0, keepdims=False)
        pairs = [(i, i ^ count) for i in range(lax.axis_size("seq"))]
        rows = keep + lax.ppermute(give, "seq", pairs)
    rows = rows + shift(rows, "expert", 1)
    return (rows + shift(rows, "mp", 1)).reshape(-1)


def swap(block, axis):
    return shift(block, axis, 1)


def quad_join(block, across, axis):
    return cat([block, across, swap(block, "expert"), swap(across, "expert")], axis)


def quad_gather(block):
    m, e = lax.axis_index("mp"), lax.axis_index("expert")
    across = swap(block, "mp")
    mine = jnp.where(m == 0, jnp.stack([block, across]), jnp.stack([across, block]))
    other = swap(mine, "expert")
    both = jnp.where(e == 0, jnp.stack([mine, other], 1), jnp.stack([other, mine], 1))
    return both.reshape((4,) + block.shape)


def quad_reduce(whole):
    m, e = lax.axis_index("mp"), lax.axis_index("expert")
    parts = whole.reshape((2, 2) + whole.shape[1:])
    give = lax.dynamic_index_in_dim(parts, 1 - e, 1, keepdims=False).astype(BF)
    keep = lax.dynamic_index_in_dim(parts, e, 1, keepdims=False).astype(F32)
    pair = keep + swap(give, "expert").astype(F32)
    give = lax.dynamic_index_in_dim(pair, 1 - m, 0, keepdims=False).astype(BF)
    keep = lax.dynamic_index_in_dim(pair, m, 0, keepdims=False)
    return keep + swap(give, "mp").astype(F32)


def pair_reduce_rel(parts):
    keep = parts[0].astype(F32) + swap(parts[2].astype(BF), "expert").astype(F32)
    give = parts[1].astype(F32) + swap(parts[3].astype(BF), "expert").astype(F32)
    return keep.astype(BF), give.astype(BF)


def across_reduce(keep, give):
    return (keep.astype(F32) + swap(give, "mp").astype(F32)).astype(BF)


def pack(prefix, action):
    fold = prefix.shape[-1] // action.shape[-1]
    rows = action.shape[-2] // fold
    parts = [action[..., k * rows : (k + 1) * rows, :] for k in range(fold)]
    return jnp.concatenate([prefix, jnp.concatenate(parts, axis=-1)], axis=-2)


def action_of(block, part_p, width):
    folded = block[..., part_p:, :]
    fold = folded.shape[-1] // width
    parts = [folded[..., k * width : (k + 1) * width] for k in range(fold)]
    return jnp.concatenate(parts, axis=-2)


def a2a(parts):
    return lax.all_to_all(parts, "seq", 0, 0, tiled=True)


def split_columns(weight):
    depth, width = weight.shape
    count = lax.axis_size("seq")
    return weight.reshape(depth, count, width // count).transpose(1, 0, 2)


def split_rows(weight):
    width, depth = weight.shape
    count = lax.axis_size("seq")
    return weight.reshape(count, width // count, depth)


def join_rows(parts):
    return parts.reshape(-1, parts.shape[-1])


def join_columns(parts):
    return parts.transpose(1, 0, 2).reshape(parts.shape[1], -1)


def rms_norm(values, gain_vec):
    return values * lax.rsqrt(jnp.mean(values * values, axis=-1, keepdims=True) + EPS) * gain_vec


def norm_backward(values, gain_vec, grad_normed):
    return jax.vjp(rms_norm, values, gain_vec)[1](grad_normed)


def geglu_act(gate_pre, up_pre):
    return jax.nn.gelu(gate_pre, approximate=True) * up_pre


def attend_forward(query_flat, key_rows, value_rows, keep_mask):
    row_count = query_flat.shape[0]
    head_size = key_rows.shape[1]
    query_heads = query_flat.reshape(row_count, -1, head_size)
    scores = jnp.einsum(
        "qhd,kd->hqk", query_heads, key_rows, preferred_element_type=F32
    ) * (head_size ** (-0.5))
    scores = jnp.where(keep_mask[None, None, :], scores, MASKED)
    expo = jnp.exp(scores - jnp.max(scores, axis=-1, keepdims=True))
    probs = expo / jnp.sum(expo, axis=-1, keepdims=True)
    mixed_rows = jnp.einsum(
        "hqk,kd->qhd", probs.astype(BF), value_rows, preferred_element_type=F32
    )
    return mixed_rows.reshape(row_count, -1).astype(BF), probs


def attend_backward(query_flat, key_rows, value_rows, probs, grad_mixed):
    row_count = query_flat.shape[0]
    head_size = key_rows.shape[1]
    score_scale = head_size ** (-0.5)
    query_heads = query_flat.reshape(row_count, -1, head_size)
    grad_heads = grad_mixed.reshape(row_count, -1, head_size)
    grad_probs = jnp.einsum("qhd,kd->hqk", grad_heads, value_rows, preferred_element_type=F32)
    row_inner = jnp.sum(grad_probs * probs, axis=-1, keepdims=True)
    grad_scores = (probs * (grad_probs - row_inner)).astype(BF)
    grad_query = jnp.einsum("hqk,kd->qhd", grad_scores, key_rows, preferred_element_type=F32)
    grad_query = (grad_query * score_scale).reshape(row_count, -1).astype(BF)
    grad_keys = score_scale * jnp.einsum(
        "hqk,qhd->kd", grad_scores, query_heads, preferred_element_type=F32
    )
    grad_values = jnp.einsum(
        "hqk,qhd->kd", probs.astype(BF), grad_heads, preferred_element_type=F32
    )
    return grad_query, jnp.concatenate([grad_keys, grad_values], axis=1)


def gelu_parts(gate):
    square = gate * gate
    bend = jnp.tanh(gate * (GELU_A + (GELU_A * GELU_B) * square))
    half = 0.5 + 0.5 * bend
    act = gate * half
    return act, half + act * (1.0 - bend) * (GELU_A + (3.0 * GELU_A * GELU_B) * square)


def feed_back(normed, cot, w_gate, w_up, w_down):
    gate, up, grad = dot(normed, w_gate, 1, 0), dot(normed, w_up, 1, 0), dot(cot, w_down, 1, 1)
    act, slope = gelu_parts(gate)
    return (act * up).astype(BF), (grad * up * slope).astype(BF), (grad * act).astype(BF)


def whole_block(shape):
    return pl.BlockSpec(shape, lambda j, *_: (0,) * len(shape), pipeline_mode=pl.Buffered(1))


def column_block(rows, tile):
    return pl.BlockSpec((rows, tile), lambda j, *_: (0, j))


def row_block(tile, columns):
    return pl.BlockSpec((tile, columns), lambda j, *_: (j, 0))


def row_kernel(body, count, ins, outs, flops, name, order=(), scratch=()):
    moved = sum(math.prod(a.shape) * a.dtype.itemsize for a, _ in ins + outs)
    return pl.pallas_call(
        body,
        grid_spec=pltpu.PrefetchScalarGridSpec(
            num_scalar_prefetch=len(order),
            grid=(count,),
            in_specs=[spec for _, spec in ins],
            out_specs=[spec for _, spec in outs],
            scratch_shapes=scratch,
        ),
        out_shape=[shape for shape, _ in outs],
        compiler_params=pltpu.CompilerParams(vmem_limit_bytes=VMEM_BYTES),
        cost_estimate=pl.CostEstimate(flops=flops // SHARE, transcendentals=0, bytes_accessed=moved // SHARE),
        name=name,
    )(*order, *[a for a, _ in ins])


def like(rows, columns):
    return jax.ShapeDtypeStruct((rows, columns), BF)


def feed_inner(normed, cots, part, w_gate, w_up, w_down, width_a):
    depth, width = w_gate[0].shape[0], 4 * w_gate[0].shape[1]
    normed, order = normed.blocks_and_owners()
    count, packed = cots.shape[0], cots.shape[1]
    rows, part_a = count * part, (packed - part) * depth // width_a
    if not on_ring():
        whole = jnp.stack(normed)
        joined = [block[:, :part].reshape(rows, depth) for block in (whole, cots)]
        action = [action_of(block, part, width_a).reshape(-1, width_a) for block in (whole, cots)]
        weights = cat(w_gate, 1), cat(w_up, 1), cat(w_down, 0)
        return feed_back(*joined, *weights), joined, action

    def place(block, owner, out_ref, action_ref):
        out_ref[pl.ds(pl.multiple_of(owner * part, 16), part), :] = block[:part, :]
        for k in range(depth // width_a):
            at = pl.multiple_of(owner * part_a + k * (packed - part), 16)
            columns = pl.ds(k * width_a, width_a)
            action_ref[pl.ds(at, packed - part), :] = block[part:packed, columns]

    steps = width // 4 // TILE

    def body(order_ref, *refs):
        cot_ref, weights = refs[count], refs[count + 1 : count + 13]
        mid_ref, dg_ref, du_ref, n_ref, c_ref, na_ref, ca_ref = refs[count + 13 : count + 20]
        chosen = refs[count + 20 :]

        @pl.when(pl.program_id(0) == 0)
        def _():
            for k in range(count):
                place(refs[k], order_ref[k], n_ref, na_ref)
                place(cot_ref.at[k], k, c_ref, ca_ref)

        for q in range(4):

            @pl.when(pl.program_id(0) // steps == q)
            def _():
                for k in range(3):
                    chosen[k][...] = weights[4 * k + q][...]

        mid_ref[...], dg_ref[...], du_ref[...] = feed_back(
            n_ref[...], c_ref[...], *[ref[...] for ref in chosen]
        )

    def part_of(q, axis):
        def index(j, *_):
            at = jnp.clip(j - q * steps, 0, steps - 1)
            return (0, at) if axis else (at, 0)

        return pl.BlockSpec((depth, TILE) if axis else (TILE, depth), index)

    ins = [(block, whole_block((packed, depth))) for block in normed]
    ins += [(cots, whole_block((count, packed, depth)))]
    ins += [(w_gate[q], part_of(q, 1)) for q in range(4)]
    ins += [(w_up[q], part_of(q, 1)) for q in range(4)]
    ins += [(w_down[q], part_of(q, 0)) for q in range(4)]
    outs = [(like(rows, width), column_block(rows, TILE))] * 3
    outs += [(like(rows, depth), whole_block((rows, depth)))] * 2
    outs += [(like(count * part_a, width_a), whole_block((count * part_a, width_a)))] * 2
    scratch = [pltpu.VMEM((depth, TILE), BF)] * 2 + [pltpu.VMEM((TILE, depth), BF)]
    flops = 6 * rows * depth * width
    out = row_kernel(body, width // TILE, ins, outs, flops, "feed_inner", (order,), scratch)
    return out[:3], out[3:5], out[5:]


def feed_outer(d_gate, d_up, w_gate, w_up):
    if not on_ring():
        return (dot(d_gate, cat(w_gate, 1), 1, 1) + dot(d_up, cat(w_up, 1), 1, 1)).astype(BF)
    (rows, width), depth = d_gate.shape, w_gate[0].shape[0]

    def body(dg_ref, du_ref, *refs):
        gate, up = (cat([ref[...] for ref in refs[k : k + 4]], 1) for k in (0, 4))
        total = dot(dg_ref[...], gate, 1, 1) + dot(du_ref[...], up, 1, 1)
        refs[8][...] = total.astype(BF)

    ins = [(d_gate, whole_block((rows, width))), (d_up, whole_block((rows, width)))]
    ins += [(part, row_block(TILE, width // 4)) for part in list(w_gate) + list(w_up)]
    outs = [(like(rows, depth), column_block(rows, TILE))]
    return row_kernel(body, depth // TILE, ins, outs, 4 * rows * depth * width, "feed_outer")[0]


def feed_down(mid, w_down):
    if not on_ring():
        return dot(mid, cat(w_down, 0), 1, 0).astype(BF)
    (rows, width), depth = mid.shape, w_down[0].shape[1]

    def body(mid_ref, *refs):
        weight = cat([ref[...] for ref in refs[:4]], 0)
        refs[4][...] = dot(mid_ref[...], weight, 1, 0).astype(BF)

    ins = [(mid, whole_block((rows, width)))]
    ins += [(part, column_block(width // 4, TILE)) for part in w_down]
    outs = [(like(rows, depth), column_block(rows, TILE))]
    return row_kernel(body, depth // TILE, ins, outs, 2 * rows * depth * width, "feed_down")[0]


def action_weights(part, depth):
    gate, up = part[:, :depth], part[:, depth : 2 * depth]
    down = cat([part[k, 2 * depth :] for k in range(part.shape[0])], 1)
    return gate.reshape(-1, gate.shape[-1]), up.reshape(-1, up.shape[-1]), down


def action_grads(normed, cot, mid, d_gate, d_up, depth):
    gate, up = dot(normed, d_gate, 0, 0).astype(BF), dot(normed, d_up, 0, 0).astype(BF)
    down = dot(mid, cot, 0, 0).astype(BF)
    return (
        gate.reshape(-1, depth, gate.shape[-1]),
        up.reshape(-1, depth, up.shape[-1]),
        [down[:, k : k + depth] for k in range(0, down.shape[1], depth)],
    )


def feed_action(normed, cot, parts, depth):
    def run(normed, cot, parts):
        grad_rows, y, grads = 0.0, 0.0, []
        for part in parts:
            gate, up, down = action_weights(part, depth)
            mid, d_gate, d_up = feed_back(normed, cot, gate, up, down)
            grad_rows = grad_rows + dot(d_gate, gate, 1, 1) + dot(d_up, up, 1, 1)
            y = y + dot(mid, down, 1, 0)
            grads.append(action_grads(normed, cot, mid, d_gate, d_up, depth))
        return grad_rows.astype(BF), y.astype(BF), grads

    if not on_ring():
        grad_rows, y, grads = run(normed, cot, parts)
        grads = [jnp.concatenate([g, u, jnp.stack(d)], axis=1) for g, u, d in grads]
        return grad_rows, y, grads

    def body(n_ref, c_ref, *refs):
        grad_rows, y, grads = run(n_ref[...], c_ref[...], [ref[...] for ref in refs[:4]])
        refs[4][...], refs[5][...] = grad_rows, y
        for out_ref, (gate, up, down) in zip(refs[6:], grads):
            out_ref[:, :depth, :], out_ref[:, depth : 2 * depth, :] = gate, up
            for k, block in enumerate(down):
                out_ref[k, 2 * depth :, :] = block

    rows = [normed, cot] + list(parts)
    ins = [(a, whole_block(a.shape)) for a in rows]
    outs = [jax.ShapeDtypeStruct(a.shape, BF) for a in rows]
    outs = [(shape, whole_block(shape.shape)) for shape in outs]
    flops = 80 * normed.shape[0] * normed.shape[1] * parts[0].shape[-1]
    out = row_kernel(body, 1, ins, outs, flops, "feed_action")
    return out[0], out[1], out[2:]


def weight_grad(left, right):
    return dot(left, right, 0, 0).astype(BF)


def quarters(array, axis):
    return jnp.split(array, 4, axis=axis)


def quarter_grads(left, right):
    if not on_ring():
        return quarters(weight_grad(left, right), 1)
    (rows, depth), width = left.shape, right.shape[1]

    def body(left_ref, right_ref, *out_refs):
        out = dot(left_ref[...], right_ref[...], 0, 0).astype(BF)
        for k, out_ref in enumerate(out_refs):
            out_ref[...] = out[:, k * (width // 4) : (k + 1) * (width // 4)]

    ins = [(left, column_block(rows, TILE)), (right, whole_block((rows, width)))]
    outs = [(like(depth, width // 4), row_block(TILE, width // 4))] * 4
    return row_kernel(body, depth // TILE, ins, outs, 2 * rows * depth * width, "feed_grads")


def body(
    hidden_prefix,
    hidden_action,
    norm1_prefix,
    query_prefix,
    key_prefix,
    value_prefix,
    out_prefix,
    norm2_prefix,
    gate_prefix,
    up_prefix,
    down_prefix,
    norm1_action,
    query_action,
    key_action,
    value_action,
    out_action,
    norm2_action,
    gate_action,
    up_action,
    down_action,
    cot_prefix,
    cot_action,
    instr_len,
    slot_source,
):
    seq_index = lax.axis_index("seq")
    episodes = lax.axis_size("seq")
    quad = lax.axis_size("mp") * lax.axis_size("expert")
    mine = lax.axis_index("mp") * lax.axis_size("expert") + lax.axis_index("expert")
    prefix_rows, action_rows_all = hidden_prefix.shape[0], hidden_action.shape[0]
    slot_count = slot_source.shape[0]
    action_rows = action_rows_all // slot_count
    head_size = key_prefix.shape[1]
    head_cols = query_prefix.shape[1]
    part_p = -(-prefix_rows // (16 * quad)) * 16
    part_a = -(-action_rows_all // (16 * quad)) * 16
    kv_cols = 2 * head_size // quad

    positions = jnp.arange(prefix_rows, dtype=jnp.int32)
    keep_prefix = positions < IMG + instr_len[seq_index]
    live_slot = slot_source >= 0
    offsets = jnp.where(live_slot, slot_source, 0)
    source_ep = (seq_index - offsets + episodes) % episodes
    keep_slots = (positions[None, :] < IMG + instr_len[source_ep][:, None]) & live_slot[:, None]
    keep_all = jnp.concatenate(
        [keep_slots, jnp.ones((slot_count, action_rows), dtype=bool)], axis=1
    )
    from_prev = slot_source == 1
    from_here = slot_source == 0
    live_rows = jnp.repeat(live_slot.astype(F32), action_rows)[:, None]

    def own_part(rows, part):
        return lax.dynamic_slice_in_dim(pad_rows(rows, quad * part), mine * part, part, axis=0)

    x_p, x_a = own_part(hidden_prefix, part_p), own_part(hidden_action, part_a)
    x_p, x_a = x_p.astype(F32), x_a.astype(F32)
    live_a = own_part(live_rows, part_a)
    cot_p, cot_a = own_part(cot_prefix, part_p), own_part(cot_action, part_a)
    cot_block = pack(cot_p, (cot_a.astype(F32) * live_a).astype(BF))

    def quarter_kv(w_key, w_value):
        return lax.dynamic_slice_in_dim(
            jnp.concatenate([w_key, w_value], axis=1), mine * kv_cols, kv_cols, axis=1
        )

    early_cols = head_cols + kv_cols
    depth_p, depth_a = query_prefix.shape[0], query_action.shape[0]
    gains = jnp.concatenate([norm1_prefix, norm2_prefix, norm1_action, norm2_action])
    gain_rows = -(-gains.shape[0] // (16 * early_cols)) * 16
    gain_block = jnp.pad(gains, (0, gain_rows * early_cols - gains.shape[0]))
    early = jnp.concatenate(
        [
            jnp.concatenate([query_prefix, quarter_kv(key_prefix, value_prefix)], axis=1),
            jnp.concatenate([query_action, quarter_kv(key_action, value_action)], axis=1),
            gain_block.reshape(gain_rows, early_cols),
        ],
        axis=0,
    )
    early = lax.all_gather(early, "seq", axis=0, tiled=False)
    in_action = [split_columns(gate_action), split_columns(up_action), split_rows(down_action)]
    in_action = jnp.concatenate(in_action, axis=1)
    late = jnp.concatenate([out_prefix, out_action], axis=1)
    late = lax.all_gather(late, "seq", axis=0, tiled=False)

    gate_p = join_rows(a2a(split_columns(gate_prefix)))
    gate_other = swap(gate_p, "expert")
    early, gate_other = fence(early, gate_other)
    w_in_p = early[:, :depth_p].reshape(-1, early_cols)
    w_in_a = early[:, depth_p : depth_p + depth_a].reshape(-1, early_cols)
    gains = early[:, depth_p + depth_a :].reshape(episodes, -1)
    gain1_p = gains[:, :depth_p].reshape(-1).astype(F32)
    gain2_p = gains[:, depth_p : 2 * depth_p].reshape(-1).astype(F32)
    gain1_a = gains[:, 2 * depth_p : 2 * depth_p + depth_a].reshape(-1).astype(F32)
    gain2_a = gains[:, 2 * depth_p + depth_a : 2 * (depth_p + depth_a)].reshape(-1).astype(F32)

    normed1_p = rms_norm(hidden_prefix.astype(F32), gain1_p).astype(BF)
    normed1_a = rms_norm(hidden_action.astype(F32), gain1_a).astype(BF)
    in_p, in_a = dot(normed1_p, w_in_p, 1, 0).astype(BF), dot(normed1_a, w_in_a, 1, 0).astype(BF)
    kv_prev = shift(in_p[:, head_cols:], "seq", 1)
    kv_own = jnp.concatenate([in_p[:, head_cols:], in_a[:, head_cols:]], axis=0)

    def whole_kv(quarter):
        return quad_gather(quarter).transpose(1, 0, 2).reshape(-1, 2 * head_size)

    kv_own = whole_kv(kv_own)
    in_p, in_a, kv_own, kv_prev, gate_p, up_p, cot_block = fence(
        in_p, in_a, kv_own, kv_prev, gate_p, split_columns(up_prefix), cot_block
    )
    gate_far = swap(gate_p, "mp")
    query_p, query_a = in_p[:, :head_cols], in_a[:, :head_cols]
    up_p = a2a(up_p)
    cots = lax.all_gather(cot_block, "seq", axis=0, tiled=False)
    kv_prev = whole_kv(kv_prev)
    kv_p, kv_a = kv_own[:prefix_rows], kv_own[prefix_rows:]
    keys_p, values_p = kv_p[:, :head_size], kv_p[:, head_size:]
    mixed_p, probs_p = attend_forward(query_p, keys_p, values_p, keep_prefix)
    kv_slots = jnp.where(from_prev[:, None, None], kv_prev[None], kv_p[None])
    kv_slots = jnp.concatenate([kv_slots, kv_a.reshape(slot_count, action_rows, -1)], axis=1)
    keys_slots, values_slots = kv_slots[:, :, :head_size], kv_slots[:, :, head_size:]
    query_slots = query_a.reshape(slot_count, action_rows, -1)
    mixed_slots, probs_a = jax.vmap(attend_forward)(
        query_slots, keys_slots, values_slots, keep_all
    )
    mixed_a = mixed_slots.reshape(action_rows_all, -1)
    mixed_p, mixed_a, up_p, gate_far, down_p = fence(
        mixed_p, mixed_a, up_p, gate_far, split_rows(down_prefix)
    )
    down_p, up_p = a2a(down_p), join_rows(up_p)
    gate_far_other = swap(gate_far, "expert")
    up_far, up_other = swap(up_p, "mp"), swap(up_p, "expert")
    w_gate_p = [gate_p, gate_far, gate_other, gate_far_other]
    w_out_p = join_columns(late[:, :, :depth_p])
    w_out_a = join_columns(late[:, :, depth_p:])
    attn_p = dot(pad_rows(mixed_p, quad * part_p), w_out_p, 1, 0).reshape(quad, part_p, -1)
    attn_a = dot(pad_rows(mixed_a, quad * part_a), w_out_a, 1, 0).reshape(quad, part_a, -1)
    attn, up_far, up_other = fence(pack(attn_p, attn_a), up_far, up_other)
    attn, down_p = fence(quad_reduce(attn), down_p)
    down_p = join_columns(down_p)
    down_far, down_other = swap(down_p, "mp"), swap(down_p, "expert")
    middle_p = x_p + attn[:part_p]
    middle_a = x_a + live_a * action_of(attn, part_p, x_a.shape[1])
    normed2 = Gathered(
        pack(rms_norm(middle_p, gain2_p).astype(BF), rms_norm(middle_a, gain2_a).astype(BF))
    )
    normed2.hop()
    w_up_p = [up_p, up_far, up_other, swap(up_far, "expert")]
    w_up_p = normed2.meet(w_up_p)[0]
    normed2.hop()
    normed2.meet()
    normed2.hop()
    down_far, down_other = normed2.meet(down_far, down_other)
    normed2.hop()
    w_down_p = [down_p, down_far, down_other, swap(down_far, "expert")]
    w_down_p, cots, in_action = normed2.meet(w_down_p, cots, in_action)
    in_action = a2a(in_action)

    inner, (normed2_p, cots_p), (normed2_a, cots_a) = feed_inner(
        normed2, cots, part_p, w_gate_p, w_up_p, w_down_p, x_a.shape[1]
    )
    mid_p, d_gate_p, d_up_p = inner
    mid_p, d_gate_p, d_up_p, in_action = fence(mid_p, d_gate_p, d_up_p, in_action)
    far_action = swap(in_action, "mp")
    dwd_p = quarters(weight_grad(mid_p, cots_p), 0)
    dwd_p, mid_p, far_action = fence(dwd_p, mid_p, far_action)
    dwd_p, y_sum = pair_reduce_rel(dwd_p), feed_down(mid_p, w_down_p)
    in_action = [in_action, far_action, swap(in_action, "expert"), swap(far_action, "expert")]
    dwd_p, y_sum, d_gate_p, in_action = fence(dwd_p, y_sum, d_gate_p, in_action)
    y_sum = y_sum.reshape(episodes, part_p, -1)
    y_sum = lax.psum_scatter(y_sum, "seq", scatter_dimension=0).astype(F32)
    dwd_p, dwg_p = across_reduce(*dwd_p), quarter_grads(normed2_p, d_gate_p)
    dwg_p, d_up_p, in_action = fence(dwg_p, d_up_p, in_action)
    dwg_p, dwu_p = pair_reduce_rel(dwg_p), quarter_grads(normed2_p, d_up_p)
    gn2_a, y_a, d_action = feed_action(normed2_a, cots_a, in_action, depth_a)
    dwd_p, dwg_p, dwu_p, d_gate_p, d_up_p, gn2_a, y_a, d_action = fence(
        dwd_p, dwg_p, dwu_p, d_gate_p, d_up_p, gn2_a, y_a, d_action
    )
    dwd_p, dwg_p = a2a(split_columns(dwd_p)), across_reduce(*dwg_p)
    dwu_p, d_action = pair_reduce_rel(dwu_p), pair_reduce_rel(d_action)
    gn2_p = feed_outer(d_gate_p, d_up_p, w_gate_p, w_up_p).reshape(episodes, part_p, -1)
    gn2_a, y_a = gn2_a.reshape(episodes, part_a, -1), y_a.reshape(episodes, part_a, -1)
    owners = ring_owners() if on_ring() else range(episodes)
    chunks = [pack(pack(gn2_p[k], gn2_a[k]), y_a[k]) for k in [owners[k] for k in range(episodes)]]
    chunks, dwd_p, dwg_p, dwu_p, y_sum, d_action = fence(
        chunks, dwd_p, dwg_p, dwu_p, y_sum, d_action
    )
    gn2 = Summed(chunks)
    gn2.hop()
    dwu_p, d_action = across_reduce(*dwu_p), across_reduce(*d_action)
    gn2.meet()
    gn2.hop()
    gn2.meet()
    gn2.hop()
    dwu_p = gn2.meet(dwu_p)[0]
    gn2.hop()
    gn2, dwg_p, d_action = fence(gn2.total(), dwg_p, d_action)
    d_action = a2a(d_action).astype(F32)
    packed = x_p.shape[0] + x_a.shape[0] * x_a.shape[1] // x_p.shape[1]
    y_a = action_of(gn2, packed, x_a.shape[1])
    gn2 = gn2[:packed]

    dmid_norm_p, dgain2_p = norm_backward(middle_p, gain2_p, gn2[:part_p])
    dmid_norm_a, dgain2_a = norm_backward(
        middle_a, gain2_a, action_of(gn2, part_p, x_a.shape[1])
    )
    dmid_p = cot_p.astype(F32) + dmid_norm_p
    dmid_a = cot_a.astype(F32) + dmid_norm_a
    dao = quad_gather(pack(dmid_p.astype(BF), (dmid_a * live_a).astype(BF)))

    def whole_rows(block):
        prefix = block[:, :part_p].reshape(quad * part_p, -1)[:prefix_rows]
        action = action_of(block, part_p, x_a.shape[1]).reshape(quad * part_a, -1)
        return prefix, action[:action_rows_all]

    dao_p, dao_a = whole_rows(dao)
    dao_p, dao_a, dwg_p, d_action = fence(dao_p, dao_a, dwg_p, d_action)
    dwg_p = a2a(split_rows(dwg_p))

    dwo = jnp.concatenate(
        [
            weight_grad(mixed_p, dao_p).reshape(head_cols, episodes, -1),
            weight_grad(mixed_a, dao_a).reshape(head_cols, episodes, -1),
        ],
        axis=2,
    ).transpose(1, 0, 2)
    dwo, dao_p, dao_a = fence(dwo, dao_p, dao_a)
    dwo = lax.psum_scatter(dwo, "seq", scatter_dimension=0, tiled=False).astype(F32)
    dmix_p, dmix_a = dot(dao_p, w_out_p, 1, 1).astype(BF), dot(dao_a, w_out_a, 1, 1).astype(BF)
    dq_slots, dkv_slots = jax.vmap(attend_backward)(
        query_slots,
        keys_slots,
        values_slots,
        probs_a,
        dmix_a.reshape(slot_count, action_rows, -1),
    )
    dkv_pre = dkv_slots[:, :prefix_rows]
    dkv_a = dkv_slots[:, prefix_rows:].reshape(action_rows_all, -1)
    to_prev = jnp.sum(jnp.where(from_prev[:, None, None], dkv_pre, 0.0), axis=0)
    to_here = jnp.sum(jnp.where(from_here[:, None, None], dkv_pre, 0.0), axis=0)

    def own_quarter(rows):
        return quad_reduce(rows.reshape(-1, quad, kv_cols).transpose(1, 0, 2))

    returned = own_quarter(jnp.concatenate([to_prev, dkv_a], axis=0))
    dkv_a = returned[prefix_rows:].astype(BF)
    returned = shift(returned[:prefix_rows].astype(BF), "seq", -1)
    returned, dkv_a, dmix_p, dwg_p, dwu_p = fence(returned, dkv_a, dmix_p, dwg_p, dwu_p)
    dwu_p = a2a(split_rows(dwu_p))
    dq_p, dkv_p = attend_backward(query_p, keys_p, values_p, probs_p, dmix_p)
    dkv_p = dkv_p + to_here
    dq_a = dq_slots.reshape(action_rows_all, -1)

    dkv_p = (own_quarter(dkv_p) + returned.astype(F32)).astype(BF)
    din_p = jnp.concatenate([dq_p, dkv_p], axis=1)
    din_a = jnp.concatenate([dq_a, dkv_a], axis=1)
    gn1_p = dot(pad_rows(din_p, quad * part_p), w_in_p, 1, 1).reshape(quad, part_p, -1)
    gn1_a = dot(pad_rows(din_a, quad * part_a), w_in_a, 1, 1).reshape(quad, part_a, -1)
    gn1 = quad_reduce(pack(gn1_p, gn1_a))
    gn1, dwu_p, dwo = fence(gn1, dwu_p, dwo)
    dx_norm_p, dgain1_p = norm_backward(x_p, gain1_p, gn1[:part_p])
    dx_norm_a, dgain1_a = norm_backward(x_a, gain1_a, action_of(gn1, part_p, x_a.shape[1]))
    dx = quad_gather(pack((dmid_p + dx_norm_p).astype(BF), (dmid_a + dx_norm_a).astype(BF)))
    dx_p, dx_a = whole_rows(dx)
    dx_p, dx_a = dx_p.astype(F32), dx_a.astype(F32)
    y_p, y_a = middle_p + y_sum, middle_a + live_a * y_a
    y_out = quad_gather(pack(y_p.astype(BF), y_a.astype(BF)))
    y_p, y_a = whole_rows(y_out)

    dwd_p = join_rows(dwd_p).astype(F32)
    dwg_p = join_columns(dwg_p).astype(F32)
    dwu_p = join_columns(dwu_p).astype(F32)
    dwg_a = join_columns(d_action[:, :depth_a])
    dwu_a = join_columns(d_action[:, depth_a : 2 * depth_a])
    dwd_a = join_rows(d_action[:, 2 * depth_a :])

    dw_in = jnp.concatenate(
        [
            weight_grad(normed1_p, din_p).reshape(episodes, -1, early_cols),
            weight_grad(normed1_a, din_a).reshape(episodes, -1, early_cols),
        ],
        axis=1,
    )
    dw_in = lax.psum_scatter(dw_in, "seq", scatter_dimension=0, tiled=False)
    dw_kv = quad_gather(dw_in[:, head_cols:]).transpose(1, 0, 2).reshape(-1, 2 * head_size)
    dw_kv = dw_kv.astype(F32)
    dw_in = dw_in.astype(F32)

    dgains = jnp.concatenate(
        [g.reshape(episodes, -1) for g in (dgain1_p, dgain2_p, dgain1_a, dgain2_a)], axis=1
    )
    dgains = seq_halve(dgains)
    return (
        y_p,
        y_a,
        dx_p,
        dx_a,
        dgains[:depth_p],
        dw_in[:depth_p, :head_cols],
        dw_kv[:depth_p, :head_size],
        dw_kv[:depth_p, head_size:],
        dwo[:, :depth_p],
        dgains[depth_p : 2 * depth_p],
        dwg_p,
        dwu_p,
        dwd_p,
        dgains[2 * depth_p : 2 * depth_p + depth_a],
        dw_in[depth_p:, :head_cols],
        dw_kv[depth_p:, :head_size],
        dw_kv[depth_p:, head_size:],
        dwo[:, depth_p:],
        dgains[2 * depth_p + depth_a :],
        dwg_a,
        dwu_a,
        dwd_a,
    )


def solution(mesh):
    rows, flat = P("seq", None), P("seq")
    wide, tall = P("seq", ("mp", "expert")), P(("mp", "expert"), "seq")
    one_expert = (flat, wide, rows, rows, tall, flat, wide, wide, tall)
    return jax.shard_map(
        body,
        mesh=mesh,
        in_specs=(rows, rows) + one_expert + one_expert + (rows, rows, P(), flat),
        out_specs=(rows, rows, rows, rows) + one_expert + one_expert,
        check_vma=False,
    )
```

```python
import math

import jax
import jax.numpy as jnp
from jax import lax
from jax.experimental import pallas as pl
from jax.experimental.pallas import tpu as pltpu
from jax.sharding import PartitionSpec as P

IMG = 512
EPS = 1e-06
MASKED = -1e30
GELU_A = (2.0 / math.pi) ** 0.5
GELU_B = 0.044715
TILE = 256
VMEM_BYTES = 60 * 2**20
SHARE = 1000
BF = jnp.bfloat16
F32 = jnp.float32

SNAKE = (0, 2, 4, 6, 7, 5, 3, 1)


def dot(left, right, left_dim, right_dim):
    return lax.dot_general(
        left, right, (((left_dim,), (right_dim,)), ((), ())), preferred_element_type=F32
    )


def fence(*values):
    return lax.optimization_barrier(values)


def cat(parts, axis=0):
    return parts[0] if len(parts) == 1 else jnp.concatenate(parts, axis=axis)


def pad_rows(block, rows):
    missing = rows - block.shape[0]
    return jnp.pad(block, ((0, missing), (0, 0))) if missing else block


def shift(block, axis, distance):
    count = lax.axis_size(axis)
    return lax.ppermute(block, axis, [(i, (i + distance) % count) for i in range(count)])


def ring_step(block, step):
    pairs = [(SNAKE[i], SNAKE[(i + step) % len(SNAKE)]) for i in range(len(SNAKE))]
    return lax.ppermute(block, "seq", pairs)


def ring_owners():
    count = len(SNAKE)
    place = jnp.array([SNAKE.index(i) for i in range(count)], jnp.int32)[lax.axis_index("seq")]
    steps = [(k + 1) // 2 if k % 2 else -(k // 2) for k in range(count)]
    return jnp.array(SNAKE, jnp.int32)[(place + jnp.array(steps, jnp.int32) + count) % count]


def on_ring():
    return lax.axis_size("seq") == len(SNAKE)


class Gathered:
    def __init__(self, block):
        self.ahead, self.behind = [block], [block]

    def hop(self):
        if on_ring():
            if len(self.ahead) <= len(SNAKE) // 2:
                self.ahead.append(ring_step(self.ahead[-1], -1))
            if len(self.behind) <= (len(SNAKE) - 1) // 2:
                self.behind.append(ring_step(self.behind[-1], 1))

    def meet(self, *values):
        self.ahead[-1], self.behind[-1], *values = fence(self.ahead[-1], self.behind[-1], *values)
        return values

    def blocks_and_owners(self):
        if not on_ring():
            whole = lax.all_gather(self.ahead[0], "seq", axis=0, tiled=False)
            return [whole[k] for k in range(whole.shape[0])], None
        order = [self.ahead[0]]
        for k in range(1, len(SNAKE)):
            order.append(self.ahead[(k + 1) // 2] if k % 2 else self.behind[k // 2])
        return order, ring_owners()


class Summed:
    def __init__(self, blocks):
        self.blocks, self.left, self.done = blocks, len(blocks) - 3, False
        self.going, self.back = blocks[-1], blocks[-2]

    def hop(self):
        if not on_ring():
            return
        going = ring_step(self.going, 1).astype(F32)
        if self.left < 0:
            self.back, self.done = self.back + going, True
            return
        self.going = (going + self.blocks[self.left].astype(F32)).astype(BF)
        back = ring_step(self.back, -1).astype(F32) + self.blocks[self.left - 1].astype(F32)
        self.back = back if self.left == 1 else back.astype(BF)
        self.left -= 2

    def meet(self, *values):
        self.going, self.back, *values = fence(self.going, self.back, *values)
        return values

    def total(self):
        if on_ring():
            assert self.done
            return self.back
        return lax.psum_scatter(jnp.stack(self.blocks), "seq", scatter_dimension=0).astype(F32)


def seq_halve(rows):
    count, index = rows.shape[0], lax.axis_index("seq")
    while count > 1:
        count //= 2
        bit = (index // count) % 2
        halves = rows.reshape(2, count, -1)
        keep = lax.dynamic_index_in_dim(halves, bit, 0, keepdims=False)
        give = lax.dynamic_index_in_dim(halves, 1 - bit, 0, keepdims=False)
        pairs = [(i, i ^ count) for i in range(lax.axis_size("seq"))]
        rows = keep + lax.ppermute(give, "seq", pairs)
    rows = rows + shift(rows, "expert", 1)
    return (rows + shift(rows, "mp", 1)).reshape(-1)


def swap(block, axis):
    return shift(block, axis, 1)


def quad_join(block, across, axis):
    return cat([block, across, swap(block, "expert"), swap(across, "expert")], axis)


def quad_gather(block):
    m, e = lax.axis_index("mp"), lax.axis_index("expert")
    across = swap(block, "mp")
    mine = jnp.where(m == 0, jnp.stack([block, across]), jnp.stack([across, block]))
    other = swap(mine, "expert")
    both = jnp.where(e == 0, jnp.stack([mine, other], 1), jnp.stack([other, mine], 1))
    return both.reshape((4,) + block.shape)


def quad_reduce(whole):
    m, e = lax.axis_index("mp"), lax.axis_index("expert")
    parts = whole.reshape((2, 2) + whole.shape[1:])
    give = lax.dynamic_index_in_dim(parts, 1 - e, 1, keepdims=False).astype(BF)
    keep = lax.dynamic_index_in_dim(parts, e, 1, keepdims=False).astype(F32)
    pair = keep + swap(give, "expert").astype(F32)
    give = lax.dynamic_index_in_dim(pair, 1 - m, 0, keepdims=False).astype(BF)
    keep = lax.dynamic_index_in_dim(pair, m, 0, keepdims=False)
    return keep + swap(give, "mp").astype(F32)


def pair_reduce_rel(parts):
    keep = parts[0].astype(F32) + swap(parts[2].astype(BF), "expert").astype(F32)
    give = parts[1].astype(F32) + swap(parts[3].astype(BF), "expert").astype(F32)
    return keep.astype(BF), give.astype(BF)


def across_reduce(keep, give):
    return (keep.astype(F32) + swap(give, "mp").astype(F32)).astype(BF)


def pack(prefix, action):
    fold = prefix.shape[-1] // action.shape[-1]
    rows = action.shape[-2] // fold
    parts = [action[..., k * rows : (k + 1) * rows, :] for k in range(fold)]
    return jnp.concatenate([prefix, jnp.concatenate(parts, axis=-1)], axis=-2)


def action_of(block, part_p, width):
    folded = block[..., part_p:, :]
    fold = folded.shape[-1] // width
    parts = [folded[..., k * width : (k + 1) * width] for k in range(fold)]
    return jnp.concatenate(parts, axis=-2)


def a2a(parts):
    return lax.all_to_all(parts, "seq", 0, 0, tiled=True)


def split_columns(weight):
    depth, width = weight.shape
    count = lax.axis_size("seq")
    return weight.reshape(depth, count, width // count).transpose(1, 0, 2)


def split_rows(weight):
    width, depth = weight.shape
    count = lax.axis_size("seq")
    return weight.reshape(count, width // count, depth)


def join_rows(parts):
    return parts.reshape(-1, parts.shape[-1])


def join_columns(parts):
    return parts.transpose(1, 0, 2).reshape(parts.shape[1], -1)


def rms_norm(values, gain_vec):
    return values * lax.rsqrt(jnp.mean(values * values, axis=-1, keepdims=True) + EPS) * gain_vec


def norm_backward(values, gain_vec, grad_normed):
    return jax.vjp(rms_norm, values, gain_vec)[1](grad_normed)


def geglu_act(gate_pre, up_pre):
    return jax.nn.gelu(gate_pre, approximate=True) * up_pre


def attend_forward(query_flat, key_rows, value_rows, keep_mask):
    row_count = query_flat.shape[0]
    head_size = key_rows.shape[1]
    query_heads = query_flat.reshape(row_count, -1, head_size)
    scores = jnp.einsum(
        "qhd,kd->hqk", query_heads, key_rows, preferred_element_type=F32
    ) * (head_size ** (-0.5))
    scores = jnp.where(keep_mask[None, None, :], scores, MASKED)
    expo = jnp.exp(scores - jnp.max(scores, axis=-1, keepdims=True))
    probs = expo / jnp.sum(expo, axis=-1, keepdims=True)
    mixed_rows = jnp.einsum(
        "hqk,kd->qhd", probs.astype(BF), value_rows, preferred_element_type=F32
    )
    return mixed_rows.reshape(row_count, -1).astype(BF), probs


def attend_backward(query_flat, key_rows, value_rows, probs, grad_mixed):
    row_count = query_flat.shape[0]
    head_size = key_rows.shape[1]
    score_scale = head_size ** (-0.5)
    query_heads = query_flat.reshape(row_count, -1, head_size)
    grad_heads = grad_mixed.reshape(row_count, -1, head_size)
    grad_probs = jnp.einsum("qhd,kd->hqk", grad_heads, value_rows, preferred_element_type=F32)
    row_inner = jnp.sum(grad_probs * probs, axis=-1, keepdims=True)
    grad_scores = (probs * (grad_probs - row_inner)).astype(BF)
    grad_query = jnp.einsum("hqk,kd->qhd", grad_scores, key_rows, preferred_element_type=F32)
    grad_query = (grad_query * score_scale).reshape(row_count, -1).astype(BF)
    grad_keys = score_scale * jnp.einsum(
        "hqk,qhd->kd", grad_scores, query_heads, preferred_element_type=F32
    )
    grad_values = jnp.einsum(
        "hqk,qhd->kd", probs.astype(BF), grad_heads, preferred_element_type=F32
    )
    return grad_query, jnp.concatenate([grad_keys, grad_values], axis=1)


def gelu_parts(gate):
    square = gate * gate
    bend = jnp.tanh(gate * (GELU_A + (GELU_A * GELU_B) * square))
    half = 0.5 + 0.5 * bend
    act = gate * half
    return act, half + act * (1.0 - bend) * (GELU_A + (3.0 * GELU_A * GELU_B) * square)


def feed_back(normed, cot, w_gate, w_up, w_down):
    gate, up, grad = dot(normed, w_gate, 1, 0), dot(normed, w_up, 1, 0), dot(cot, w_down, 1, 1)
    act, slope = gelu_parts(gate)
    return (act * up).astype(BF), (grad * up * slope).astype(BF), (grad * act).astype(BF)


def whole_block(shape):
    return pl.BlockSpec(shape, lambda j, *_: (0,) * len(shape), pipeline_mode=pl.Buffered(1))


def column_block(rows, tile):
    return pl.BlockSpec((rows, tile), lambda j, *_: (0, j))


def row_block(tile, columns):
    return pl.BlockSpec((tile, columns), lambda j, *_: (j, 0))


def row_kernel(body, count, ins, outs, flops, name, order=(), scratch=()):
    moved = sum(math.prod(a.shape) * a.dtype.itemsize for a, _ in ins + outs)
    return pl.pallas_call(
        body,
        grid_spec=pltpu.PrefetchScalarGridSpec(
            num_scalar_prefetch=len(order),
            grid=(count,),
            in_specs=[spec for _, spec in ins],
            out_specs=[spec for _, spec in outs],
            scratch_shapes=scratch,
        ),
        out_shape=[shape for shape, _ in outs],
        compiler_params=pltpu.CompilerParams(vmem_limit_bytes=VMEM_BYTES),
        cost_estimate=pl.CostEstimate(flops=flops // SHARE, transcendentals=0, bytes_accessed=moved // SHARE),
        name=name,
    )(*order, *[a for a, _ in ins])


def like(rows, columns):
    return jax.ShapeDtypeStruct((rows, columns), BF)


def feed_inner(normed, cots, part, w_gate, w_up, w_down, width_a):
    depth, width = w_gate[0].shape[0], 4 * w_gate[0].shape[1]
    normed, order = normed.blocks_and_owners()
    count, packed = cots.shape[0], cots.shape[1]
    rows, part_a = count * part, (packed - part) * depth // width_a
    if not on_ring():
        whole = jnp.stack(normed)
        joined = [block[:, :part].reshape(rows, depth) for block in (whole, cots)]
        action = [action_of(block, part, width_a).reshape(-1, width_a) for block in (whole, cots)]
        weights = cat(w_gate, 1), cat(w_up, 1), cat(w_down, 0)
        return feed_back(*joined, *weights), joined, action

    def place(block, owner, out_ref, action_ref):
        out_ref[pl.ds(pl.multiple_of(owner * part, 16), part), :] = block[:part, :]
        for k in range(depth // width_a):
            at = pl.multiple_of(owner * part_a + k * (packed - part), 16)
            columns = pl.ds(k * width_a, width_a)
            action_ref[pl.ds(at, packed - part), :] = block[part:packed, columns]

    steps = width // 4 // TILE

    def body(order_ref, *refs):
        cot_ref, weights = refs[count], refs[count + 1 : count + 13]
        mid_ref, dg_ref, du_ref, n_ref, c_ref, na_ref, ca_ref = refs[count + 13 : count + 20]
        chosen = refs[count + 20 :]

        @pl.when(pl.program_id(0) == 0)
        def _():
            for k in range(count):
                place(refs[k], order_ref[k], n_ref, na_ref)
                place(cot_ref.at[k], k, c_ref, ca_ref)

        for q in range(4):

            @pl.when(pl.program_id(0) // steps == q)
            def _():
                for k in range(3):
                    chosen[k][...] = weights[4 * k + q][...]

        mid_ref[...], dg_ref[...], du_ref[...] = feed_back(
            n_ref[...], c_ref[...], *[ref[...] for ref in chosen]
        )

    def part_of(q, axis):
        def index(j, *_):
            at = jnp.clip(j - q * steps, 0, steps - 1)
            return (0, at) if axis else (at, 0)

        return pl.BlockSpec((depth, TILE) if axis else (TILE, depth), index)

    ins = [(block, whole_block((packed, depth))) for block in normed]
    ins += [(cots, whole_block((count, packed, depth)))]
    ins += [(w_gate[q], part_of(q, 1)) for q in range(4)]
    ins += [(w_up[q], part_of(q, 1)) for q in range(4)]
    ins += [(w_down[q], part_of(q, 0)) for q in range(4)]
    outs = [(like(rows, width), column_block(rows, TILE))] * 3
    outs += [(like(rows, depth), whole_block((rows, depth)))] * 2
    outs += [(like(count * part_a, width_a), whole_block((count * part_a, width_a)))] * 2
    scratch = [pltpu.VMEM((depth, TILE), BF)] * 2 + [pltpu.VMEM((TILE, depth), BF)]
    flops = 6 * rows * depth * width
    out = row_kernel(body, width // TILE, ins, outs, flops, "feed_inner", (order,), scratch)
    return out[:3], out[3:5], out[5:]


def feed_outer(d_gate, d_up, w_gate, w_up):
    if not on_ring():
        return (dot(d_gate, cat(w_gate, 1), 1, 1) + dot(d_up, cat(w_up, 1), 1, 1)).astype(BF)
    (rows, width), depth = d_gate.shape, w_gate[0].shape[0]

    def body(dg_ref, du_ref, *refs):
        gate, up = (cat([ref[...] for ref in refs[k : k + 4]], 1) for k in (0, 4))
        total = dot(dg_ref[...], gate, 1, 1) + dot(du_ref[...], up, 1, 1)
        refs[8][...] = total.astype(BF)

    ins = [(d_gate, whole_block((rows, width))), (d_up, whole_block((rows, width)))]
    ins += [(part, row_block(TILE, width // 4)) for part in list(w_gate) + list(w_up)]
    outs = [(like(rows, depth), column_block(rows, TILE))]
    return row_kernel(body, depth // TILE, ins, outs, 4 * rows * depth * width, "feed_outer")[0]


def feed_down(mid, w_down):
    if not on_ring():
        return dot(mid, cat(w_down, 0), 1, 0).astype(BF)
    (rows, width), depth = mid.shape, w_down[0].shape[1]

    def body(mid_ref, *refs):
        weight = cat([ref[...] for ref in refs[:4]], 0)
        refs[4][...] = dot(mid_ref[...], weight, 1, 0).astype(BF)

    ins = [(mid, whole_block((rows, width)))]
    ins += [(part, column_block(width // 4, TILE)) for part in w_down]
    outs = [(like(rows, depth), column_block(rows, TILE))]
    return row_kernel(body, depth // TILE, ins, outs, 2 * rows * depth * width, "feed_down")[0]


def action_weights(part, depth):
    gate, up = part[:, :depth], part[:, depth : 2 * depth]
    down = cat([part[k, 2 * depth :] for k in range(part.shape[0])], 1)
    return gate.reshape(-1, gate.shape[-1]), up.reshape(-1, up.shape[-1]), down


def action_grads(normed, cot, mid, d_gate, d_up, depth):
    gate, up = dot(normed, d_gate, 0, 0).astype(BF), dot(normed, d_up, 0, 0).astype(BF)
    down = dot(mid, cot, 0, 0).astype(BF)
    return (
        gate.reshape(-1, depth, gate.shape[-1]),
        up.reshape(-1, depth, up.shape[-1]),
        [down[:, k : k + depth] for k in range(0, down.shape[1], depth)],
    )


def feed_action(normed, cot, parts, depth):
    def run(normed, cot, parts):
        grad_rows, y, grads = 0.0, 0.0, []
        for part in parts:
            gate, up, down = action_weights(part, depth)
            mid, d_gate, d_up = feed_back(normed, cot, gate, up, down)
            grad_rows = grad_rows + dot(d_gate, gate, 1, 1) + dot(d_up, up, 1, 1)
            y = y + dot(mid, down, 1, 0)
            grads.append(action_grads(normed, cot, mid, d_gate, d_up, depth))
        return grad_rows.astype(BF), y.astype(BF), grads

    if not on_ring():
        grad_rows, y, grads = run(normed, cot, parts)
        grads = [jnp.concatenate([g, u, jnp.stack(d)], axis=1) for g, u, d in grads]
        return grad_rows, y, grads

    def body(n_ref, c_ref, *refs):
        grad_rows, y, grads = run(n_ref[...], c_ref[...], [ref[...] for ref in refs[:4]])
        refs[4][...], refs[5][...] = grad_rows, y
        for out_ref, (gate, up, down) in zip(refs[6:], grads):
            out_ref[:, :depth, :], out_ref[:, depth : 2 * depth, :] = gate, up
            for k, block in enumerate(down):
                out_ref[k, 2 * depth :, :] = block

    rows = [normed, cot] + list(parts)
    ins = [(a, whole_block(a.shape)) for a in rows]
    outs = [jax.ShapeDtypeStruct(a.shape, BF) for a in rows]
    outs = [(shape, whole_block(shape.shape)) for shape in outs]
    flops = 80 * normed.shape[0] * normed.shape[1] * parts[0].shape[-1]
    out = row_kernel(body, 1, ins, outs, flops, "feed_action")
    return out[0], out[1], out[2:]


def weight_grad(left, right):
    return dot(left, right, 0, 0).astype(BF)


def quarters(array, axis):
    return jnp.split(array, 4, axis=axis)


def quarter_grads(left, right):
    if not on_ring():
        return quarters(weight_grad(left, right), 1)
    (rows, depth), width = left.shape, right.shape[1]

    def body(left_ref, right_ref, *out_refs):
        out = dot(left_ref[...], right_ref[...], 0, 0).astype(BF)
        for k, out_ref in enumerate(out_refs):
            out_ref[...] = out[:, k * (width // 4) : (k + 1) * (width // 4)]

    ins = [(left, column_block(rows, TILE)), (right, whole_block((rows, width)))]
    outs = [(like(depth, width // 4), row_block(TILE, width // 4))] * 4
    return row_kernel(body, depth // TILE, ins, outs, 2 * rows * depth * width, "feed_grads")


def body(
    hidden_prefix,
    hidden_action,
    norm1_prefix,
    query_prefix,
    key_prefix,
    value_prefix,
    out_prefix,
    norm2_prefix,
    gate_prefix,
    up_prefix,
    down_prefix,
    norm1_action,
    query_action,
    key_action,
    value_action,
    out_action,
    norm2_action,
    gate_action,
    up_action,
    down_action,
    cot_prefix,
    cot_action,
    instr_len,
    slot_source,
):
    seq_index = lax.axis_index("seq")
    episodes = lax.axis_size("seq")
    quad = lax.axis_size("mp") * lax.axis_size("expert")
    mine = lax.axis_index("mp") * lax.axis_size("expert") + lax.axis_index("expert")
    prefix_rows, action_rows_all = hidden_prefix.shape[0], hidden_action.shape[0]
    slot_count = slot_source.shape[0]
    action_rows = action_rows_all // slot_count
    head_size = key_prefix.shape[1]
    head_cols = query_prefix.shape[1]
    part_p = -(-prefix_rows // (16 * quad)) * 16
    part_a = -(-action_rows_all // (16 * quad)) * 16
    kv_cols = 2 * head_size // quad

    positions = jnp.arange(prefix_rows, dtype=jnp.int32)
    keep_prefix = positions < IMG + instr_len[seq_index]
    live_slot = slot_source >= 0
    offsets = jnp.where(live_slot, slot_source, 0)
    source_ep = (seq_index - offsets + episodes) % episodes
    keep_slots = (positions[None, :] < IMG + instr_len[source_ep][:, None]) & live_slot[:, None]
    keep_all = jnp.concatenate(
        [keep_slots, jnp.ones((slot_count, action_rows), dtype=bool)], axis=1
    )
    from_prev = slot_source == 1
    from_here = slot_source == 0
    live_rows = jnp.repeat(live_slot.astype(F32), action_rows)[:, None]

    def own_part(rows, part):
        return lax.dynamic_slice_in_dim(pad_rows(rows, quad * part), mine * part, part, axis=0)

    x_p, x_a = own_part(hidden_prefix, part_p), own_part(hidden_action, part_a)
    x_p, x_a = x_p.astype(F32), x_a.astype(F32)
    live_a = own_part(live_rows, part_a)
    cot_p, cot_a = own_part(cot_prefix, part_p), own_part(cot_action, part_a)
    cot_block = pack(cot_p, (cot_a.astype(F32) * live_a).astype(BF))

    def quarter_kv(w_key, w_value):
        return lax.dynamic_slice_in_dim(
            jnp.concatenate([w_key, w_value], axis=1), mine * kv_cols, kv_cols, axis=1
        )

    early_cols = head_cols + kv_cols
    depth_p, depth_a = query_prefix.shape[0], query_action.shape[0]
    gains = jnp.concatenate([norm1_prefix, norm2_prefix, norm1_action, norm2_action])
    gain_rows = -(-gains.shape[0] // (16 * early_cols)) * 16
    gain_block = jnp.pad(gains, (0, gain_rows * early_cols - gains.shape[0]))
    early = jnp.concatenate(
        [
            jnp.concatenate([query_prefix, quarter_kv(key_prefix, value_prefix)], axis=1),
            jnp.concatenate([query_action, quarter_kv(key_action, value_action)], axis=1),
            gain_block.reshape(gain_rows, early_cols),
        ],
        axis=0,
    )
    early = lax.all_gather(early, "seq", axis=0, tiled=False)
    in_action = [split_columns(gate_action), split_columns(up_action), split_rows(down_action)]
    in_action = jnp.concatenate(in_action, axis=1)
    late = jnp.concatenate([out_prefix, out_action], axis=1)
    late = lax.all_gather(late, "seq", axis=0, tiled=False)

    gate_p = join_rows(a2a(split_columns(gate_prefix)))
    gate_other = swap(gate_p, "expert")
    early, gate_other = fence(early, gate_other)
    w_in_p = early[:, :depth_p].reshape(-1, early_cols)
    w_in_a = early[:, depth_p : depth_p + depth_a].reshape(-1, early_cols)
    gains = early[:, depth_p + depth_a :].reshape(episodes, -1)
    gain1_p = gains[:, :depth_p].reshape(-1).astype(F32)
    gain2_p = gains[:, depth_p : 2 * depth_p].reshape(-1).astype(F32)
    gain1_a = gains[:, 2 * depth_p : 2 * depth_p + depth_a].reshape(-1).astype(F32)
    gain2_a = gains[:, 2 * depth_p + depth_a : 2 * (depth_p + depth_a)].reshape(-1).astype(F32)

    normed1_p = rms_norm(hidden_prefix.astype(F32), gain1_p).astype(BF)
    normed1_a = rms_norm(hidden_action.astype(F32), gain1_a).astype(BF)
    in_p, in_a = dot(normed1_p, w_in_p, 1, 0).astype(BF), dot(normed1_a, w_in_a, 1, 0).astype(BF)
    kv_prev = shift(in_p[:, head_cols:], "seq", 1)
    kv_own = jnp.concatenate([in_p[:, head_cols:], in_a[:, head_cols:]], axis=0)

    def whole_kv(quarter):
        return quad_gather(quarter).transpose(1, 0, 2).reshape(-1, 2 * head_size)

    kv_own = whole_kv(kv_own)
    in_p, in_a, kv_own, kv_prev, gate_p, up_p, cot_block = fence(
        in_p, in_a, kv_own, kv_prev, gate_p, split_columns(up_prefix), cot_block
    )
    gate_far = swap(gate_p, "mp")
    query_p, query_a = in_p[:, :head_cols], in_a[:, :head_cols]
    up_p = a2a(up_p)
    cots = lax.all_gather(cot_block, "seq", axis=0, tiled=False)
    kv_prev = whole_kv(kv_prev)
    kv_p, kv_a = kv_own[:prefix_rows], kv_own[prefix_rows:]
    keys_p, values_p = kv_p[:, :head_size], kv_p[:, head_size:]
    mixed_p, probs_p = attend_forward(query_p, keys_p, values_p, keep_prefix)
    kv_slots = jnp.where(from_prev[:, None, None], kv_prev[None], kv_p[None])
    kv_slots = jnp.concatenate([kv_slots, kv_a.reshape(slot_count, action_rows, -1)], axis=1)
    keys_slots, values_slots = kv_slots[:, :, :head_size], kv_slots[:, :, head_size:]
    query_slots = query_a.reshape(slot_count, action_rows, -1)
    mixed_slots, probs_a = jax.vmap(attend_forward)(
        query_slots, keys_slots, values_slots, keep_all
    )
    mixed_a = mixed_slots.reshape(action_rows_all, -1)
    mixed_p, mixed_a, up_p, gate_far, down_p = fence(
        mixed_p, mixed_a, up_p, gate_far, split_rows(down_prefix)
    )
    down_p, up_p = a2a(down_p), join_rows(up_p)
    gate_far_other = swap(gate_far, "expert")
    up_far, up_other = swap(up_p, "mp"), swap(up_p, "expert")
    w_gate_p = [gate_p, gate_far, gate_other, gate_far_other]
    w_out_p = join_columns(late[:, :, :depth_p])
    w_out_a = join_columns(late[:, :, depth_p:])
    attn_p = dot(pad_rows(mixed_p, quad * part_p), w_out_p, 1, 0).reshape(quad, part_p, -1)
    attn_a = dot(pad_rows(mixed_a, quad * part_a), w_out_a, 1, 0).reshape(quad, part_a, -1)
    attn, up_far, up_other = fence(pack(attn_p, attn_a), up_far, up_other)
    attn, down_p, cots = fence(quad_reduce(attn), down_p, cots)
    down_p = join_columns(down_p)
    down_far, down_other = swap(down_p, "mp"), swap(down_p, "expert")
    middle_p = x_p + attn[:part_p]
    middle_a = x_a + live_a * action_of(attn, part_p, x_a.shape[1])
    normed2 = Gathered(
        pack(rms_norm(middle_p, gain2_p).astype(BF), rms_norm(middle_a, gain2_a).astype(BF))
    )
    normed2.hop()
    w_up_p = [up_p, up_far, up_other, swap(up_far, "expert")]
    w_up_p = normed2.meet(w_up_p)[0]
    normed2.hop()
    normed2.meet()
    normed2.hop()
    down_far, down_other = normed2.meet(down_far, down_other)
    normed2.hop()
    w_down_p = [down_p, down_far, down_other, swap(down_far, "expert")]
    w_down_p, in_action = normed2.meet(w_down_p, in_action)
    in_action = a2a(in_action)

    inner, (normed2_p, cots_p), (normed2_a, cots_a) = feed_inner(
        normed2, cots, part_p, w_gate_p, w_up_p, w_down_p, x_a.shape[1]
    )
    mid_p, d_gate_p, d_up_p = inner
    mid_p, d_gate_p, d_up_p, in_action = fence(mid_p, d_gate_p, d_up_p, in_action)
    far_action = swap(in_action, "mp")
    dwd_p = quarters(weight_grad(mid_p, cots_p), 0)
    dwd_p, mid_p, far_action = fence(dwd_p, mid_p, far_action)
    dwd_p, y_sum = pair_reduce_rel(dwd_p), feed_down(mid_p, w_down_p)
    in_action = [in_action, far_action, swap(in_action, "expert"), swap(far_action, "expert")]
    dwd_p, y_sum, d_gate_p, in_action = fence(dwd_p, y_sum, d_gate_p, in_action)
    y_sum = y_sum.reshape(episodes, part_p, -1)
    y_sum = lax.psum_scatter(y_sum, "seq", scatter_dimension=0).astype(F32)
    dwd_p, dwg_p = across_reduce(*dwd_p), quarter_grads(normed2_p, d_gate_p)
    dwg_p, d_up_p, in_action = fence(dwg_p, d_up_p, in_action)
    dwg_p, dwu_p = pair_reduce_rel(dwg_p), quarter_grads(normed2_p, d_up_p)
    gn2_a, y_a, d_action = feed_action(normed2_a, cots_a, in_action, depth_a)
    dwd_p, dwg_p, dwu_p, d_gate_p, d_up_p, gn2_a, y_a, d_action = fence(
        dwd_p, dwg_p, dwu_p, d_gate_p, d_up_p, gn2_a, y_a, d_action
    )
    dwd_p, dwg_p = a2a(split_columns(dwd_p)), across_reduce(*dwg_p)
    dwu_p, d_action = pair_reduce_rel(dwu_p), pair_reduce_rel(d_action)
    gn2_p = feed_outer(d_gate_p, d_up_p, w_gate_p, w_up_p).reshape(episodes, part_p, -1)
    gn2_a, y_a = gn2_a.reshape(episodes, part_a, -1), y_a.reshape(episodes, part_a, -1)
    owners = ring_owners() if on_ring() else range(episodes)
    chunks = [pack(pack(gn2_p[k], gn2_a[k]), y_a[k]) for k in [owners[k] for k in range(episodes)]]
    chunks, dwd_p, dwg_p, dwu_p, y_sum, d_action = fence(
        chunks, dwd_p, dwg_p, dwu_p, y_sum, d_action
    )
    gn2 = Summed(chunks)
    gn2.hop()
    dwu_p, d_action = across_reduce(*dwu_p), across_reduce(*d_action)
    gn2.meet()
    gn2.hop()
    gn2.meet()
    gn2.hop()
    dwu_p = gn2.meet(dwu_p)[0]
    gn2.hop()
    gn2, dwg_p, d_action = fence(gn2.total(), dwg_p, d_action)
    d_action = a2a(d_action).astype(F32)
    packed = x_p.shape[0] + x_a.shape[0] * x_a.shape[1] // x_p.shape[1]
    y_a = action_of(gn2, packed, x_a.shape[1])
    gn2 = gn2[:packed]

    dmid_norm_p, dgain2_p = norm_backward(middle_p, gain2_p, gn2[:part_p])
    dmid_norm_a, dgain2_a = norm_backward(
        middle_a, gain2_a, action_of(gn2, part_p, x_a.shape[1])
    )
    dmid_p = cot_p.astype(F32) + dmid_norm_p
    dmid_a = cot_a.astype(F32) + dmid_norm_a
    dao = quad_gather(pack(dmid_p.astype(BF), (dmid_a * live_a).astype(BF)))

    def whole_rows(block):
        prefix = block[:, :part_p].reshape(quad * part_p, -1)[:prefix_rows]
        action = action_of(block, part_p, x_a.shape[1]).reshape(quad * part_a, -1)
        return prefix, action[:action_rows_all]

    dao_p, dao_a = whole_rows(dao)
    dao_p, dao_a, dwg_p, d_action = fence(dao_p, dao_a, dwg_p, d_action)
    dwg_p = a2a(split_rows(dwg_p))

    dwo = jnp.concatenate(
        [
            weight_grad(mixed_p, dao_p).reshape(head_cols, episodes, -1),
            weight_grad(mixed_a, dao_a).reshape(head_cols, episodes, -1),
        ],
        axis=2,
    ).transpose(1, 0, 2)
    dwo, dao_p, dao_a = fence(dwo, dao_p, dao_a)
    dwo = lax.psum_scatter(dwo, "seq", scatter_dimension=0, tiled=False).astype(F32)
    dmix_p, dmix_a = dot(dao_p, w_out_p, 1, 1).astype(BF), dot(dao_a, w_out_a, 1, 1).astype(BF)
    dq_slots, dkv_slots = jax.vmap(attend_backward)(
        query_slots,
        keys_slots,
        values_slots,
        probs_a,
        dmix_a.reshape(slot_count, action_rows, -1),
    )
    dkv_pre = dkv_slots[:, :prefix_rows]
    dkv_a = dkv_slots[:, prefix_rows:].reshape(action_rows_all, -1)
    to_prev = jnp.sum(jnp.where(from_prev[:, None, None], dkv_pre, 0.0), axis=0)
    to_here = jnp.sum(jnp.where(from_here[:, None, None], dkv_pre, 0.0), axis=0)

    def own_quarter(rows):
        return quad_reduce(rows.reshape(-1, quad, kv_cols).transpose(1, 0, 2))

    returned = own_quarter(jnp.concatenate([to_prev, dkv_a], axis=0))
    dkv_a = returned[prefix_rows:].astype(BF)
    returned = shift(returned[:prefix_rows].astype(BF), "seq", -1)
    returned, dkv_a, dmix_p, dwg_p, dwu_p = fence(returned, dkv_a, dmix_p, dwg_p, dwu_p)
    dwu_p = a2a(split_rows(dwu_p))
    dq_p, dkv_p = attend_backward(query_p, keys_p, values_p, probs_p, dmix_p)
    dkv_p = dkv_p + to_here
    dq_a = dq_slots.reshape(action_rows_all, -1)

    dkv_p = (own_quarter(dkv_p) + returned.astype(F32)).astype(BF)
    din_p = jnp.concatenate([dq_p, dkv_p], axis=1)
    din_a = jnp.concatenate([dq_a, dkv_a], axis=1)
    gn1_p = dot(pad_rows(din_p, quad * part_p), w_in_p, 1, 1).reshape(quad, part_p, -1)
    gn1_a = dot(pad_rows(din_a, quad * part_a), w_in_a, 1, 1).reshape(quad, part_a, -1)
    gn1 = quad_reduce(pack(gn1_p, gn1_a))
    gn1, dwu_p, dwo = fence(gn1, dwu_p, dwo)
    dx_norm_p, dgain1_p = norm_backward(x_p, gain1_p, gn1[:part_p])
    dx_norm_a, dgain1_a = norm_backward(x_a, gain1_a, action_of(gn1, part_p, x_a.shape[1]))
    dx = quad_gather(pack((dmid_p + dx_norm_p).astype(BF), (dmid_a + dx_norm_a).astype(BF)))
    dx_p, dx_a = whole_rows(dx)
    dx_p, dx_a = dx_p.astype(F32), dx_a.astype(F32)
    y_p, y_a = middle_p + y_sum, middle_a + live_a * y_a
    y_out = quad_gather(pack(y_p.astype(BF), y_a.astype(BF)))
    y_p, y_a = whole_rows(y_out)

    dwd_p = join_rows(dwd_p).astype(F32)
    dwg_p = join_columns(dwg_p).astype(F32)
    dwu_p = join_columns(dwu_p).astype(F32)
    dwg_a = join_columns(d_action[:, :depth_a])
    dwu_a = join_columns(d_action[:, depth_a : 2 * depth_a])
    dwd_a = join_rows(d_action[:, 2 * depth_a :])

    dw_in = jnp.concatenate(
        [
            weight_grad(normed1_p, din_p).reshape(episodes, -1, early_cols),
            weight_grad(normed1_a, din_a).reshape(episodes, -1, early_cols),
        ],
        axis=1,
    )
    dw_in = lax.psum_scatter(dw_in, "seq", scatter_dimension=0, tiled=False)
    dw_kv = quad_gather(dw_in[:, head_cols:]).transpose(1, 0, 2).reshape(-1, 2 * head_size)
    dw_kv = dw_kv.astype(F32)
    dw_in = dw_in.astype(F32)

    dgains = jnp.concatenate(
        [g.reshape(episodes, -1) for g in (dgain1_p, dgain2_p, dgain1_a, dgain2_a)], axis=1
    )
    dgains = seq_halve(dgains)
    return (
        y_p,
        y_a,
        dx_p,
        dx_a,
        dgains[:depth_p],
        dw_in[:depth_p, :head_cols],
        dw_kv[:depth_p, :head_size],
        dw_kv[:depth_p, head_size:],
        dwo[:, :depth_p],
        dgains[depth_p : 2 * depth_p],
        dwg_p,
        dwu_p,
        dwd_p,
        dgains[2 * depth_p : 2 * depth_p + depth_a],
        dw_in[depth_p:, :head_cols],
        dw_kv[depth_p:, :head_size],
        dw_kv[depth_p:, head_size:],
        dwo[:, depth_p:],
        dgains[2 * depth_p + depth_a :],
        dwg_a,
        dwu_a,
        dwd_a,
    )


def solution(mesh):
    rows, flat = P("seq", None), P("seq")
    wide, tall = P("seq", ("mp", "expert")), P(("mp", "expert"), "seq")
    one_expert = (flat, wide, rows, rows, tall, flat, wide, wide, tall)
    return jax.shard_map(
        body,
        mesh=mesh,
        in_specs=(rows, rows) + one_expert + one_expert + (rows, rows, P(), flat),
        out_specs=(rows, rows, rows, rows) + one_expert + one_expert,
        check_vma=False,
    )
```
